32 devices in a mesh: don: 4 (over x, core), acc: 8 (over z, y).
Axes of the slice: x: 2, y: 2, z: 4, core: 2. Of those that a mesh axis runs over, the one named last changes fastest.
Arguments:
- donor_emb: bfloat16 [65536, 768], P(('don', 'acc')), may hold values from -12 to 12
- acceptor_emb: bfloat16 [65536, 768], P(('don', 'acc')), may hold values from -6 to 6
- donor_pos: int32 [768], P(('don', 'acc')), may hold values from 0 to 2047
- acceptor_pos: int32 [768], P(('don', 'acc')), may hold values from 0 to 2047
- donor_count: int32 [32], P('don'), may hold values from 1 to 24, as said below
- acceptor_count: int32 [32], replicated, may hold values from 1 to 24, as said below
- target: int32 [64, 768], P(None, 'don'), may hold values from 0 to 767, as said below
- junction_mask: int32 [64, 768], P(None, 'don'), may hold values 0 or 1
- weights: bfloat16 [64, 768, 768], P('acc'), may hold values from -1 to 2
Outputs:
- loss: float32 [], replicated
- grad_weight: float32 [768, 64, 768], P('don', 'acc')
The draws below stay inside these ranges and needn't reach their ends.
Inputs may be any that keep to these rules, and one draw needn't show every extreme that they name: `donor_count`: the live donor slots of all shards number exactly 400; some shard has all 24 live. `acceptor_count`: the live acceptor slots of all shards number exactly 400; some shard has all 24 live. `target`: each entry names a live acceptor slot.
All inputs are finite; a program needn't handle non-finite values. No bound on the sum of `junction_mask` on one device may be relied on, other than what follows from the above.
Results may differ from the reference program's by a relative error of at most 0.0031.
Values may be sent and summed in bfloat16 or wider, within the bound.
A program may use at most 128 MiB of HBM per device.

```python
import jax
import jax.numpy as jnp
from jax import lax

D = 768
TIS = 64
CAP = 24
POS_DEV = 2048
SHARDS = 32
SEQ = 65536
DONORS = 768


def site_counts(key):
    bias_key, noise_key, chosen_key = jax.random.split(key, 3)
    extra = CAP - 1
    slots = SHARDS * extra
    needed = SHARDS * (CAP + 1) // 2 - SHARDS
    bias = jax.random.randint(bias_key, (SHARDS,), 0, 8)
    chosen = jax.random.randint(chosen_key, (), 0, SHARDS)
    bias = jnp.where(jnp.arange(SHARDS) == chosen, 12, bias)
    noise = jax.random.randint(noise_key, (SHARDS, extra), 0, 65536)
    score = noise + bias[:, None] * 16384
    order = jnp.arange(slots, dtype=jnp.int32).reshape(SHARDS, extra)
    keyed = (score * slots + order).reshape(-1).astype(jnp.int32)
    threshold = jnp.sort(keyed)[slots - needed]
    taken = (keyed >= threshold).astype(jnp.int32).reshape(SHARDS, extra)
    return (1 + jnp.sum(taken, axis=1)).astype(jnp.int32)


def draw_donor_count(key, part):
    return site_counts(jax.random.fold_in(key, 3))


def draw_acceptor_count(key, part):
    return site_counts(jax.random.fold_in(key, 5))


def draw_target(key, part):
    counts = site_counts(jax.random.fold_in(key, 5))
    shard_key, slot_key = jax.random.split(jax.random.fold_in(key, 11))
    shard = jax.random.randint(shard_key, (TIS, DONORS), 0, SHARDS)
    within = jax.random.randint(slot_key, (TIS, DONORS), 0, counts[shard])
    return (shard * CAP + within).astype(jnp.int32)


def draw_donor_emb(key, part):
    noise_key = jax.random.fold_in(jax.random.fold_in(key, 21), 0)
    values = jax.random.truncated_normal(noise_key, -6.0, 6.0, (SEQ, D), jnp.float32)
    return values.astype(jnp.bfloat16)


def draw_acceptor_emb(key, part):
    noise_key = jax.random.fold_in(key, 23)
    values = jax.random.truncated_normal(noise_key, -6.0, 6.0, (SEQ, D), jnp.float32)
    return values.astype(jnp.bfloat16)


def draw_weights(key, part):
    values = jax.random.truncated_normal(jax.random.fold_in(key, 31), -4.0, 4.0, (TIS, D, D), jnp.float32) * D ** (-0.5)
    return values.astype(jnp.bfloat16)


def touch_ends(drawn, stream_key, low, high):
    extent = drawn.shape
    spot = [jax.random.randint(jax.random.fold_in(stream_key, axis), (), 0, extent[axis]) for axis in range(len(extent))]
    drawn = drawn.at[tuple(spot)].set(low)
    longest = extent.index(max(extent))
    spot[longest] = (spot[longest] + 1) % extent[longest]
    return drawn.at[tuple(spot)].set(high)


def setup_inputs(seed: int = 0) -> dict:
    key_list = jax.random.split(jax.random.key(seed), 10)
    return {
        "donor_emb": draw_donor_emb(jax.random.fold_in(key_list[9], 71), 0),
        "acceptor_emb": draw_acceptor_emb(jax.random.fold_in(key_list[9], 71), 0),
        "donor_pos": touch_ends(jax.random.randint(key_list[2], (DONORS,), 0, POS_DEV), jax.random.fold_in(key_list[2], 1), 0, POS_DEV - 1).astype(jnp.int32),
        "acceptor_pos": touch_ends(jax.random.randint(key_list[3], (DONORS,), 0, POS_DEV), jax.random.fold_in(key_list[3], 1), 0, POS_DEV - 1).astype(jnp.int32),
        "donor_count": draw_donor_count(jax.random.fold_in(key_list[9], 71), 0),
        "acceptor_count": draw_acceptor_count(jax.random.fold_in(key_list[9], 71), 0),
        "target": draw_target(jax.random.fold_in(key_list[9], 71), 0),
        "junction_mask": touch_ends((jax.random.randint(key_list[7], (TIS, DONORS), 0, 2) < 1).astype(jnp.int32), jax.random.fold_in(key_list[7], 1), 0, 1),
        "weights": draw_weights(jax.random.fold_in(key_list[9], 71), 0),
    }


def site_rows(emb, positions):
    slot = jnp.arange(positions.shape[0], dtype=jnp.int32)
    rows = ((slot // CAP) * POS_DEV + positions).astype(jnp.int32)
    return jnp.take(emb, rows, axis=0)


def live_slots(counts):
    slot = jnp.arange(DONORS, dtype=jnp.int32)
    return (slot % CAP) < jnp.repeat(counts, CAP)


def reference(donor_emb, acceptor_emb, donor_pos, acceptor_pos, donor_count, acceptor_count, target, junction_mask, weights):
    donors = site_rows(donor_emb, donor_pos)
    acceptors = site_rows(acceptor_emb, acceptor_pos)
    live_d = live_slots(donor_count)
    live_a = live_slots(acceptor_count)
    scale = D ** -0.5
    columns = jnp.arange(DONORS, dtype=jnp.int32)

    def tissue(inputs):
        matrix, target_row, mask_row = inputs
        projected = jnp.dot(donors, matrix, preferred_element_type=jnp.float32).astype(jnp.bfloat16)
        scores = jnp.dot(projected, acceptors.T, preferred_element_type=jnp.float32) * scale
        scores = jnp.where(live_a[None, :], scores, -1e30)
        highest = jnp.max(scores, axis=1, keepdims=True)
        summed_exp = jnp.sum(jnp.where(live_a[None, :], jnp.exp(scores - highest), 0.0), axis=1, keepdims=True)
        log_total = highest + jnp.log(summed_exp)
        is_target = columns[None, :] == target_row[:, None]
        picked = jnp.sum(jnp.where(is_target, scores, 0.0), axis=1)
        weight = jnp.where(live_d, mask_row, 0).astype(jnp.float32)
        summed = jnp.sum(weight * (log_total[:, 0] - picked))
        counted = jnp.sum(weight)
        probs = jnp.where(live_a[None, :], jnp.exp(scores - log_total), 0.0)
        dscore = (weight[:, None] * (probs - is_target.astype(jnp.float32))).astype(jnp.bfloat16)
        dproj = (jnp.dot(dscore, acceptors, preferred_element_type=jnp.float32) * scale).astype(jnp.bfloat16)
        gradient = jnp.dot(donors.T, dproj, preferred_element_type=jnp.float32)
        return summed, counted, gradient

    summed, counted, gradient = lax.map(tissue, (weights, target, junction_mask))
    loss = jnp.sum(summed) / jnp.maximum(jnp.sum(counted), 1.0)
    return loss, jnp.transpose(gradient, (1, 0, 2))
```

```python
import functools

import jax
import jax.numpy as jnp
from jax import lax
from jax.experimental import pallas as pl
from jax.experimental.pallas import tpu as pltpu
from jax.sharding import PartitionSpec as P

BF16 = jnp.bfloat16
F32 = jnp.float32
I32 = jnp.int32
MESH = pl.DeviceIdType.MESH
LOG2E = 1.4426950408889634


def round_up(n, m):
    return (n + m - 1) // m * m


def row_chunk(n, limit=512):
    best = 128
    for r in range(128, limit + 1, 128):
        if n % r == 0:
            best = r
    return best


def contract_last(a, b):
    return lax.dot_general(a, b, (((1,), (1,)), ((), ())), preferred_element_type=F32)


def acceptor_tables(counts, shards, slots, width):
    col = lax.broadcasted_iota(I32, (8, width), 1)

    def step(k, carry):
        first, rank, label = carry
        number = counts[k]
        within = col - k * slots
        live = (within >= 0) & (within < number)
        rank = jnp.where(live, first + within, rank)
        last = first + number
        return last, rank, label + jnp.where(col >= last, slots - number, 0)

    return lax.fori_loop(0, shards, step, (jnp.int32(0), jnp.full((8, width), -1, I32), col))[1:]


def main_kernel(
    don_size, acc_size, inner, live,
    dpos, apos, dcnt, acnt, demb, aemb, target, mask, weights,
    tot_out, a_out, loss_out,
    demb_v, aemb_v, w_s, tm_s, xd, xa, comb_s, comb_l, cnt_s, cnt_l,
    d_s, dt_s, a_s, p_s, ds_s, tot_s, rank_s, label_s, tab_s, first_s, loss_s, loss_l,
    in_sem, send_sem, recv_sem, sib_send, sib_recv, side_send, side_recv,
    tot_send, tot_recv, loss_send, loss_recv, out_sem,
):
    shards, slots, width = xd.shape
    outer, chips = acc_size // inner, don_size // 2
    sites = shards * slots
    don_sites = sites // don_size
    half, rows_d = w_s.shape[0], d_s.shape[0]
    rows_a = a_s.shape[0]
    depth = width // don_size
    tis = 2 * half
    scale = width ** (-0.5)
    alternate = chips == inner
    don, acc = lax.axis_index("don"), lax.axis_index("acc")
    core, x = lax.rem(don, 2), don // 2
    o, i = acc // inner, lax.rem(acc, inner)
    if alternate:
        b = core * x + (1 - core) * i
        c = core * i + (1 - core) * x
        b_size, c_size = inner, inner
    else:
        b, c, b_size, c_size = i, x, inner, chips

    def place(oo, bb, cc):
        if alternate:
            xx = core * bb + (1 - core) * cc
            ii = core * cc + (1 - core) * bb
        else:
            xx, ii = cc, bb
        return (xx * 2 + core, oo * inner + ii)

    def away(at, k, size):
        return lax.rem(at + k, size)

    def slot_of(at):
        return at[0] * acc_size + at[1]

    sibling = (x * 2 + 1 - core, acc)

    tile_rows = tm_s.shape[1]
    row_at = pl.multiple_of(acc * tis // tile_rows * tile_rows, tile_rows)
    copies = [
        pltpu.make_async_copy(demb, demb_v, in_sem.at[0]),
        pltpu.make_async_copy(target.at[pl.ds(row_at, tile_rows), :], tm_s.at[0], in_sem.at[1]),
        pltpu.make_async_copy(mask.at[pl.ds(row_at, tile_rows), :], tm_s.at[1], in_sem.at[2]),
        pltpu.make_async_copy(aemb, aemb_v, in_sem.at[3]),
        pltpu.make_async_copy(weights.at[pl.ds(core * half, half)], w_s, in_sem.at[4]),
    ]
    for copy in copies:
        copy.start()

    others = [(away(don, k, don_size), acc) for k in range(1, don_size)]
    lossers = [
        (x * 2 + away(core, kc, 2), away(acc, ka, acc_size))
        for kc in range(2) for ka in range(acc_size) if kc or ka
    ]
    far = [
        (away(x, k, chips) * 2 + kc, acc) for k in range(1, chips) for kc in range(2)
    ]
    barrier = pltpu.get_barrier_semaphore()
    for peer in lossers + far:
        pl.semaphore_signal(barrier, inc=1, device_id=peer, device_id_type=MESH)

    rank_a, label_a = acceptor_tables(acnt, shards, slots, sites)
    rank_s[...] = rank_a
    label_s[...] = label_a
    lane = lax.broadcasted_iota(I32, (1, 128), 1)
    counts = jnp.zeros((1, 128), F32)
    for k in range(shards // don_size):
        counts = jnp.where(lane == don * (shards // don_size) + k, dcnt[k].astype(F32), counts)
    cnt_s[...] = jnp.broadcast_to(counts, cnt_s.shape)
    shard_row = lax.broadcasted_iota(I32, (first_s.shape[1], sites), 0)
    slot_lane = lax.broadcasted_iota(I32, (first_s.shape[1], sites), 1)
    before = slot_lane >= (shard_row + 1) * slots
    within_shard = (slot_lane >= shard_row * slots) & jnp.logical_not(before)
    first_s[0] = jnp.where(before, 1.0, 0.0).astype(BF16)
    first_s[1] = jnp.where(within_shard, 1.0, 0.0).astype(BF16)

    def own_rows(pos, emb_v, landing):
        bases = emb_v.shape[0]
        row = lax.broadcasted_iota(I32, (slots, 128), 0)
        want = jnp.zeros((slots, 128), I32)
        for k in range(slots):
            want = jnp.where(row == k, pos[k], want)
        col = lax.broadcasted_iota(I32, (slots, bases), 1)
        pick = jnp.where(col == jnp.concatenate([want] * (bases // 128), axis=1), 1.0, 0.0).astype(BF16)
        landing[held] = jnp.dot(pick, emb_v[...], preferred_element_type=F32).astype(BF16)

    held = don * acc_size + acc
    copies[0].wait()
    own_rows(dpos, demb_v, xd)
    copies[1].wait()
    copies[2].wait()
    both = tm_s[0] * 2 + tm_s[1]
    for core_at in range(2):
        mine = both[core_at * half : (core_at + 1) * half]
        for k in range(1, tile_rows // tis):
            at = k * tis + core_at * half
            mine = jnp.where(lax.rem(acc, tile_rows // tis) == k, both[at : at + half], mine)
        comb_s[core_at] = mine

    pl.semaphore_wait(barrier, len(lossers) + len(far))

    sent = []
    land = (xd, xa)

    def send(kind, source, slot, peer, count):
        n = count[kind]
        count[kind] += 1
        copy = pltpu.make_async_remote_copy(
            src_ref=source, dst_ref=land[kind].at[slot],
            send_sem=send_sem.at[kind, n], recv_sem=recv_sem.at[kind, slot],
            device_id=peer, device_id_type=MESH,
        )
        copy.start()
        sent.append(copy)

    def arrived(kind, slot):
        pltpu.make_async_copy(land[kind].at[slot], land[kind].at[slot], recv_sem.at[kind, slot]).wait()

    counter = [0, 0]

    def forward(kind, slot, hops):
        source = land[kind].at[slot]
        if hops >= 3:
            for k in range(1, outer):
                send(kind, source, slot, place(away(o, k, outer), b, c), counter)
        if hops >= 2:
            for k in range(1, b_size):
                send(kind, source, slot, place(o, away(b, k, b_size), c), counter)
        if hops >= 1:
            for k in range(1, c_size):
                send(kind, source, slot, place(o, b, away(c, k, c_size)), counter)
        send(kind, source, slot, sibling, counter)

    forward(0, held, 3)
    side = []
    for k, peer in enumerate(others):
        to = lax.rem(peer[0], 2)
        for j, (source, dest) in enumerate(((comb_s.at[to], comb_l.at[don]), (cnt_s, cnt_l.at[don]))):
            copy = pltpu.make_async_remote_copy(
                src_ref=source, dst_ref=dest, send_sem=side_send.at[k, j], recv_sem=side_recv.at[k, j],
                device_id=peer, device_id_type=MESH,
            )
            copy.start()
            side.append(copy)
    comb_l[don] = comb_s[core]
    cnt_l[don] = cnt_s[...]
    copies[3].wait()
    own_rows(apos, aemb_v, xa)
    forward(1, held, 3)

    def relay(kind, slot, hops):
        arrived(kind, slot)
        forward(kind, slot, hops)

    def stage_one(kind):
        for ko in range(1, outer):
            relay(kind, slot_of(place(away(o, ko, outer), b, c)), 2)
        for kb in range(1, b_size):
            relay(kind, slot_of(place(o, away(b, kb, b_size), c)), 1)

    def stage_two(kind):
        for ko in range(1, outer):
            for kb in range(1, b_size):
                relay(kind, slot_of(place(away(o, ko, outer), away(b, kb, b_size), c)), 1)

    def stage_three(kind):
        for kb in range(b_size):
            for ko in range(outer):
                for kc in range(1, c_size):
                    relay(kind, slot_of(place(away(o, ko, outer), away(b, kb, b_size), away(c, kc, c_size))), 0)

    def stage_four(kind):
        for kx in range(chips):
            for ka in range(acc_size):
                arrived(kind, slot_of((away(x, kx, chips) * 2 + 1 - core, away(acc, ka, acc_size))))

    stage_one(0)
    stage_one(1)
    stage_two(0)
    stage_three(0)
    stage_two(1)
    stage_three(1)

    for copy in side:
        copy.wait()
    counts = cnt_l[0]
    for k in range(1, don_size):
        counts = counts + cnt_l[k]
    counts = counts.astype(BF16)
    first = jnp.dot(counts, first_s[0], preferred_element_type=F32)
    number = jnp.dot(counts, first_s[1], preferred_element_type=F32)
    shard_of = jnp.sum(first_s[0].astype(F32), axis=0, keepdims=True)
    within = lax.broadcasted_iota(I32, (8, sites), 1).astype(F32) - shard_of * slots
    rank_d = jnp.where(within < number, first + within, -1.0).astype(I32)[:1]
    comb = jnp.concatenate([comb_l[k] for k in range(don_size)], axis=1)
    table = jnp.concatenate(
        [(comb & 1).astype(F32), ((comb >> 1) & 255).astype(F32), (comb >> 9).astype(F32)], axis=0
    ).astype(BF16)
    stage_four(0)
    chunk_d = row_chunk(rows_d)
    for n in range(rows_d // chunk_d):
        span = slice(n * chunk_d, (n + 1) * chunk_d)
        row = lax.broadcasted_iota(I32, (chunk_d, sites), 0) + n * chunk_d
        pick = jnp.where(row == rank_d, 1.0, 0.0).astype(BF16)
        d = jnp.dot(pick, xd[...].reshape(sites, width), preferred_element_type=F32)
        d_s[span, :] = d.astype(BF16)
        dt_s[:, span] = jnp.transpose(d).astype(BF16)
        tab_s[:, span] = contract_last(table, pick)
    copies[4].wait()
    for t in range(half):
        for n in range(rows_d // chunk_d):
            span = slice(n * chunk_d, (n + 1) * chunk_d)
            p_s[t, span, :] = jnp.dot(d_s[span, :], w_s[t], preferred_element_type=F32).astype(BF16)

    stage_four(1)
    chunk_a = row_chunk(rows_a)
    for n in range(rows_a // chunk_a):
        span = slice(n * chunk_a, (n + 1) * chunk_a)
        row = lax.broadcasted_iota(I32, (chunk_a, sites), 0) + n * chunk_a
        pick = jnp.where(row == rank_s[:1, :], 1.0, 0.0).astype(BF16)
        a_s[span, :] = jnp.dot(pick, xa[...].reshape(sites, width), preferred_element_type=F32).astype(BF16)
    outs = [pltpu.make_async_copy(a_s, a_out, out_sem.at[0])]
    outs[0].start()

    rows_live = round_up(live, 16)
    label_col = jnp.transpose(
        jnp.broadcast_to(label_s[:1, :rows_a].astype(F32), (128, rows_a))
    )[:rows_live]
    lost = jnp.zeros((1, rows_d), F32)
    weighed = jnp.zeros((1, rows_d), F32)
    if rows_a > rows_live:
        for t in range(half):
            ds_s[t, rows_live:, :] = jnp.zeros((rows_a - rows_live, rows_d), BF16)
    lost_parts = []
    chunk_s = row_chunk(rows_d)
    for t in range(half):
        for n in range(rows_d // chunk_s):
            span = slice(n * chunk_s, (n + 1) * chunk_s)
            raw = contract_last(a_s[:rows_live, :], p_s[t, span, :])
            if rows_live > live:
                row = lax.broadcasted_iota(I32, raw.shape, 0)
                raw = jnp.where(row < live, raw, -1e30)
            weight = tab_s[t : t + 1, span]
            goal = tab_s[half + t : half + t + 1, span] + 256.0 * tab_s[2 * half + t : 2 * half + t + 1, span]
            highest = jnp.max(raw, axis=0, keepdims=True)
            expo = jnp.exp2((raw - highest) * (scale * LOG2E))
            summed = jnp.sum(expo, axis=0, keepdims=True)
            hit = jnp.concatenate([label_col] * (chunk_s // 128), axis=1) == goal
            picked = jnp.sum(jnp.where(hit, raw, 0.0), axis=0, keepdims=True)
            lost_parts.append((weight, jnp.log(summed) + scale * (highest - picked)))
            prob = expo * (weight / summed)
            ds_s[t, :rows_live, span] = jnp.where(hit, prob - weight, prob).astype(BF16)
    num = sum(jnp.sum(w * l) for w, l in lost_parts)
    cnt = sum(jnp.sum(w) for w, l in lost_parts)
    first_row = lax.broadcasted_iota(I32, loss_s.shape, 0) == 0
    loss_s[...] = jnp.where(first_row, num, cnt)
    at_loss = core * acc_size + acc
    loss_copies = []
    for k, peer in enumerate(lossers):
        copy = pltpu.make_async_remote_copy(
            src_ref=loss_s, dst_ref=loss_l.at[at_loss], send_sem=loss_send.at[k], recv_sem=loss_recv.at[k],
            device_id=peer, device_id_type=MESH,
        )
        copy.start()
        loss_copies.append(copy)
    loss_l[at_loss] = loss_s[...]

    tot_copies = []
    for t in range(half):
        for which in range(2):
            at = pl.multiple_of((x * 2 + which) * depth, depth)
            total = contract_last(dt_s[pl.ds(at, depth), :], ds_s[t]) * scale
            tot_s[which, t] = total.astype(BF16)
        at = core * half + t
        own = pltpu.make_async_copy(tot_s.at[core, t], tot_out.at[at], out_sem.at[1 + t])
        own.start()
        outs.append(own)
        copy = pltpu.make_async_remote_copy(
            src_ref=tot_s.at[1 - core, t], dst_ref=tot_out.at[at], send_sem=tot_send.at[t], recv_sem=tot_recv.at[t],
            device_id=sibling, device_id_type=MESH,
        )
        copy.start()
        tot_copies.append(copy)

    for copy in loss_copies:
        copy.wait()
    total = loss_l[0]
    for k in range(1, 2 * acc_size):
        total = total + loss_l[k]
    loss_out[...] = jnp.broadcast_to(total[:1] / jnp.maximum(total[1:2], 1.0), loss_out.shape)
    for copy in sent:
        copy.wait_send()
    for copy in tot_copies + outs:
        copy.wait()


def main(don_size, acc_size, dpos, apos, dcnt, acnt, demb, aemb, target, mask, weights):
    slots, width = dpos.shape[0], demb.shape[1]
    tis = weights.shape[0]
    half = tis // 2
    shards = don_size * acc_size
    sites = shards * slots
    live = shards * (slots + 1) // 2
    padded = round_up(live, 128)
    depth = width // don_size
    inner = 1
    while (2 * inner) ** 2 <= acc_size:
        inner *= 2
    outer, chips = acc_size // inner, don_size // 2
    same = shards // 2
    sends = (outer - 1) + outer * (inner - 1) + outer * inner * (chips - 1) + same
    tile_rows = max(8, tis)
    smem = pl.BlockSpec(memory_space=pltpu.SMEM)
    hbm = pl.BlockSpec(memory_space=pl.ANY)
    vmem = pl.BlockSpec(memory_space=pltpu.VMEM)
    dma = pltpu.SemaphoreType.DMA
    lossers = 2 * acc_size - 1
    return pl.pallas_call(
        functools.partial(main_kernel, don_size, acc_size, inner, live),
        in_specs=[smem] * 4 + [hbm] * 5,
        out_specs=[hbm, hbm, vmem],
        out_shape=[
            jax.ShapeDtypeStruct((tis, depth, padded), BF16),
            jax.ShapeDtypeStruct((padded, width), BF16),
            jax.ShapeDtypeStruct((8, 128), F32),
        ],
        scratch_shapes=[
            pltpu.VMEM(demb.shape, BF16),
            pltpu.VMEM(aemb.shape, BF16),
            pltpu.VMEM((half, width, width), BF16),
            pltpu.VMEM((2, tile_rows, sites // don_size), I32),
            pltpu.VMEM((shards, slots, width), BF16),
            pltpu.VMEM((shards, slots, width), BF16),
            pltpu.VMEM((2, half, sites // don_size), I32),
            pltpu.VMEM((don_size, half, sites // don_size), I32),
            pltpu.VMEM((8, 128), F32),
            pltpu.VMEM((don_size, 8, 128), F32),
            pltpu.VMEM((padded, width), BF16),
            pltpu.VMEM((width, padded), BF16),
            pltpu.VMEM((padded, width), BF16),
            pltpu.VMEM((half, padded, width), BF16),
            pltpu.VMEM((half, padded, padded), BF16),
            pltpu.VMEM((2, half, depth, padded), BF16),
            pltpu.VMEM((8, sites), I32),
            pltpu.VMEM((8, sites), I32),
            pltpu.VMEM((3 * half, padded), F32),
            pltpu.VMEM((2, 128, sites), BF16),
            pltpu.VMEM((8, 128), F32),
            pltpu.VMEM((2 * acc_size, 8, 128), F32),
            dma((5,)),
            dma((2, sends)),
            dma((2, shards)),
            dma((1,)),
            dma((1,)),
            dma((don_size - 1, 2)),
            dma((don_size - 1, 2)),
            dma((half,)),
            dma((half,)),
            dma((lossers,)),
            dma((lossers,)),
            dma((1 + half,)),
        ],
        compiler_params=pltpu.CompilerParams(
            collective_id=0, has_side_effects=True, vmem_limit_bytes=60 * 1024 * 1024
        ),
    )(dpos, apos, dcnt, acnt, demb, aemb, target, mask, weights)


def grad_kernel(tot_ref, a_ref, grad_ref, buf, sem):
    copies = []
    for t in range(tot_ref.shape[0]):
        buf[t] = jnp.dot(tot_ref[t], a_ref[...], preferred_element_type=F32)
        copy = pltpu.make_async_copy(buf.at[t], grad_ref.at[:, t, :], sem.at[t])
        copy.start()
        copies.append(copy)
    for copy in copies:
        copy.wait()


def grad(total, a):
    tis, depth, _ = total.shape
    width = a.shape[1]
    vmem = pl.BlockSpec(memory_space=pltpu.VMEM)
    return pl.pallas_call(
        grad_kernel,
        in_specs=[vmem, vmem],
        out_specs=pl.BlockSpec(memory_space=pl.ANY),
        out_shape=jax.ShapeDtypeStruct((depth, tis, width), F32),
        scratch_shapes=[pltpu.VMEM((tis, depth, width), F32), pltpu.SemaphoreType.DMA((tis,))],
        compiler_params=pltpu.CompilerParams(vmem_limit_bytes=60 * 1024 * 1024),
    )(total, a)


def local(
    don_size, acc_size, donor_emb, acceptor_emb, donor_pos, acceptor_pos, donor_count, acceptor_count,
    target, junction_mask, weights,
):
    total, a, loss = main(
        don_size, acc_size, donor_pos, acceptor_pos, donor_count, acceptor_count,
        donor_emb, acceptor_emb, target, junction_mask, weights,
    )
    return loss[0, 0], grad(total, a)


def solution(mesh):
    return jax.shard_map(
        functools.partial(local, mesh.shape["don"], mesh.shape["acc"]),
        mesh=mesh,
        in_specs=(
            P(("don", "acc"), None),
            P(("don", "acc"), None),
            P(("don", "acc")),
            P(("don", "acc")),
            P("don"),
            P(),
            P(None, "don"),
            P(None, "don"),
            P("acc", None, None),
        ),
        out_specs=(P(), P("don", "acc", None)),
        check_vma=False,
    )
```

```python
import functools

import jax
import jax.numpy as jnp
from jax import lax
from jax.experimental import pallas as pl
from jax.experimental.pallas import tpu as pltpu
from jax.sharding import PartitionSpec as P

BF16 = jnp.bfloat16
F32 = jnp.float32
I32 = jnp.int32
MESH = pl.DeviceIdType.MESH
LOG2E = 1.4426950408889634


def round_up(n, m):
    return (n + m - 1) // m * m


def row_chunk(n, limit=512):
    best = 128
    for r in range(128, limit + 1, 128):
        if n % r == 0:
            best = r
    return best


def contract_last(a, b):
    return lax.dot_general(a, b, (((1,), (1,)), ((), ())), preferred_element_type=F32)


def acceptor_tables(counts, shards, slots, width):
    col = lax.broadcasted_iota(I32, (8, width), 1)

    def step(k, carry):
        first, rank, label = carry
        number = counts[k]
        within = col - k * slots
        live = (within >= 0) & (within < number)
        rank = jnp.where(live, first + within, rank)
        last = first + number
        return last, rank, label + jnp.where(col >= last, slots - number, 0)

    return lax.fori_loop(0, shards, step, (jnp.int32(0), jnp.full((8, width), -1, I32), col))[1:]


def main_kernel(
    don_size, acc_size, inner, live,
    dpos_h, apos_h, dcnt_h, acnt_h, demb, aemb, target, mask, weights,
    tot_out, a_s, loss_out,
    dpos, apos, dcnt, acnt, demb_v, aemb_v, w_s, tm_s, xd, xa, comb_s, comb_l, cnt_s, cnt_l,
    d_s, dt_s, p_s, e_s, ds_s, tot_s, rank_s, label_s, tab_s, first_s, loss_s, loss_l,
    in_sem, send_sem, recv_sem, sib_send, sib_recv, side_send, side_recv,
    tot_send, tot_recv, loss_send, loss_recv,
):
    shards, slots, width = xd.shape
    outer, chips = acc_size // inner, don_size // 2
    sites = shards * slots
    don_sites = sites // don_size
    half, rows_d = w_s.shape[0], d_s.shape[0]
    rows_a = a_s.shape[0]
    depth = width // don_size
    tis = 2 * half
    scale = width ** (-0.5)
    alternate = chips == inner
    don, acc = lax.axis_index("don"), lax.axis_index("acc")
    core, x = lax.rem(don, 2), don // 2
    o, i = acc // inner, lax.rem(acc, inner)
    if alternate:
        b = core * x + (1 - core) * i
        c = core * i + (1 - core) * x
        b_size, c_size = inner, inner
    else:
        b, c, b_size, c_size = i, x, inner, chips

    def place(oo, bb, cc):
        if alternate:
            xx = core * bb + (1 - core) * cc
            ii = core * cc + (1 - core) * bb
        else:
            xx, ii = cc, bb
        return (xx * 2 + core, oo * inner + ii)

    def away(at, k, size):
        return lax.rem(at + k, size)

    def near(at, k, size):
        up = k - 1 + jnp.where(k - 1 >= at, 1, 0)
        down = k - 1 + jnp.where(k - 1 >= size - 1 - at, 1, 0)
        return jnp.where(2 * at < size, up, size - 1 - down)

    def slot_of(at):
        return at[0] * acc_size + at[1]

    sibling = (x * 2 + 1 - core, acc)

    tile_rows = tm_s.shape[1]
    row_at = pl.multiple_of(acc * tis // tile_rows * tile_rows, tile_rows)
    copies = [
        pltpu.make_async_copy(demb, demb_v, in_sem.at[0]),
        pltpu.make_async_copy(target.at[pl.ds(row_at, tile_rows), :], tm_s.at[0], in_sem.at[1]),
        pltpu.make_async_copy(mask.at[pl.ds(row_at, tile_rows), :], tm_s.at[1], in_sem.at[2]),
        pltpu.make_async_copy(aemb, aemb_v, in_sem.at[3]),
        pltpu.make_async_copy(weights.at[pl.ds(core * half, half)], w_s, in_sem.at[4]),
    ]
    small = [
        pltpu.make_async_copy(source, dest, in_sem.at[5 + k])
        for k, (source, dest) in enumerate(((dpos_h, dpos), (apos_h, apos), (dcnt_h, dcnt), (acnt_h, acnt)))
    ]
    for copy in small + copies:
        copy.start()

    others = [(away(don, k, don_size), acc) for k in range(1, don_size)]
    lossers = [
        (x * 2 + away(core, kc, 2), away(acc, ka, acc_size))
        for kc in range(2) for ka in range(acc_size) if kc or ka
    ]
    far = [
        (away(x, k, chips) * 2 + kc, acc) for k in range(1, chips) for kc in range(2)
    ]
    barrier = pltpu.get_barrier_semaphore()
    for peer in lossers + far:
        pl.semaphore_signal(barrier, inc=1, device_id=peer, device_id_type=MESH)

    for copy in small:
        copy.wait()
    rank_a, label_a = acceptor_tables(acnt, shards, slots, sites)
    rank_s[...] = rank_a
    label_s[...] = label_a
    lane = lax.broadcasted_iota(I32, (1, 128), 1)
    counts = jnp.zeros((1, 128), F32)
    for k in range(shards // don_size):
        counts = jnp.where(lane == don * (shards // don_size) + k, dcnt[k].astype(F32), counts)
    cnt_s[...] = jnp.broadcast_to(counts, cnt_s.shape)
    shard_row = lax.broadcasted_iota(I32, (first_s.shape[1], sites), 0)
    slot_lane = lax.broadcasted_iota(I32, (first_s.shape[1], sites), 1)
    before = slot_lane >= (shard_row + 1) * slots
    within_shard = (slot_lane >= shard_row * slots) & jnp.logical_not(before)
    first_s[0] = jnp.where(before, 1.0, 0.0).astype(BF16)
    first_s[1] = jnp.where(within_shard, 1.0, 0.0).astype(BF16)

    rows_live = round_up(live, 16)
    chunk = row_chunk(rows_d)
    if rows_a > rows_live:
        a_s[rows_live:, :] = jnp.zeros((rows_a - rows_live, width), BF16)
        d_s[rows_live:, :] = jnp.zeros((rows_d - rows_live, width), BF16)
        tab_s[:, rows_live:] = jnp.zeros((tab_s.shape[0], rows_d - rows_live), F32)
        for t in range(half):
            p_s[t, rows_live:, :] = jnp.zeros((rows_d - rows_live, width), BF16)
        for t in range(ds_s.shape[0]):
            ds_s[t, rows_live:, :] = jnp.zeros((rows_a - rows_live, rows_d), BF16)

    def own_rows(pos, emb_v, landing):
        bases = emb_v.shape[0]
        row = lax.broadcasted_iota(I32, (slots, 128), 0)
        want = jnp.zeros((slots, 128), I32)
        for k in range(slots):
            want = jnp.where(row == k, pos[k], want)
        col = lax.broadcasted_iota(I32, (slots, bases), 1)
        pick = jnp.where(col == jnp.concatenate([want] * (bases // 128), axis=1), 1.0, 0.0).astype(BF16)
        landing[held] = jnp.dot(pick, emb_v[...], preferred_element_type=F32).astype(BF16)

    held = don * acc_size + acc
    copies[0].wait()
    own_rows(dpos, demb_v, xd)
    copies[1].wait()
    copies[2].wait()
    both = tm_s[0] * 2 + tm_s[1]
    for core_at in range(2):
        mine = both[core_at * half : (core_at + 1) * half]
        for k in range(1, tile_rows // tis):
            at = k * tis + core_at * half
            mine = jnp.where(lax.rem(acc, tile_rows // tis) == k, both[at : at + half], mine)
        comb_s[core_at] = mine

    pl.semaphore_wait(barrier, len(lossers) + len(far))

    sent = []
    land = (xd, xa)

    def send(kind, source, slot, peer, count):
        n = count[kind]
        count[kind] += 1
        copy = pltpu.make_async_remote_copy(
            src_ref=source, dst_ref=land[kind].at[slot],
            send_sem=send_sem.at[kind, n], recv_sem=recv_sem.at[kind, slot],
            device_id=peer, device_id_type=MESH,
        )
        copy.start()
        sent.append(copy)

    def arrived(kind, slot):
        pltpu.make_async_copy(land[kind].at[slot], land[kind].at[slot], recv_sem.at[kind, slot]).wait()

    counter = [0, 0]

    def forward(kind, slot, hops):
        source = land[kind].at[slot]
        if hops >= 3:
            for k in range(outer - 1, 0, -1):
                send(kind, source, slot, place(near(o, k, outer), b, c), counter)
        if hops >= 2:
            for k in range(1, b_size):
                send(kind, source, slot, place(o, away(b, k, b_size), c), counter)
        if hops >= 1:
            for k in range(1, c_size):
                send(kind, source, slot, place(o, b, away(c, k, c_size)), counter)
        send(kind, source, slot, sibling, counter)

    forward(0, held, 3)
    side = []
    for k, peer in enumerate(others):
        to = lax.rem(peer[0], 2)
        for j, (source, dest) in enumerate(((comb_s.at[to], comb_l.at[don]), (cnt_s, cnt_l.at[don]))):
            copy = pltpu.make_async_remote_copy(
                src_ref=source, dst_ref=dest, send_sem=side_send.at[k, j], recv_sem=side_recv.at[k, j],
                device_id=peer, device_id_type=MESH,
            )
            copy.start()
            side.append(copy)
    comb_l[don] = comb_s[core]
    cnt_l[don] = cnt_s[...]
    copies[3].wait()
    own_rows(apos, aemb_v, xa)
    forward(1, held, 3)

    def relay(kind, slot, hops):
        arrived(kind, slot)
        forward(kind, slot, hops)

    def far_o(ko):
        return near(o, ko, outer) if ko else o

    def stage_one(kind):
        for kb in range(1, b_size):
            relay(kind, slot_of(place(o, away(b, kb, b_size), c)), 1)
        for ko in range(1, outer):
            relay(kind, slot_of(place(far_o(ko), b, c)), 2)

    def stage_two(kind):
        for ko in range(1, outer):
            for kb in range(1, b_size):
                relay(kind, slot_of(place(far_o(ko), away(b, kb, b_size), c)), 1)

    def stage_three(kind, own_b):
        for ko in range(outer):
            for kb in range(1) if own_b else range(1, b_size):
                for kc in range(1, c_size):
                    relay(kind, slot_of(place(far_o(ko), away(b, kb, b_size), away(c, kc, c_size))), 0)

    def stage_four(kind):
        for kx in range(chips):
            for ka in range(acc_size):
                arrived(kind, slot_of((away(x, kx, chips) * 2 + 1 - core, away(acc, ka, acc_size))))

    stage_one(0)
    stage_one(1)
    stage_two(0)
    stage_three(0, True)
    stage_two(1)
    stage_three(0, False)
    stage_three(1, True)

    for copy in side:
        copy.wait()
    counts = cnt_l[0]
    for k in range(1, don_size):
        counts = counts + cnt_l[k]
    counts = counts.astype(BF16)
    first = jnp.dot(counts, first_s[0], preferred_element_type=F32)
    number = jnp.dot(counts, first_s[1], preferred_element_type=F32)
    shard_of = jnp.sum(first_s[0].astype(F32), axis=0, keepdims=True)
    within = lax.broadcasted_iota(I32, (8, sites), 1).astype(F32) - shard_of * slots
    rank_d = jnp.where(within < number, first + within, -1.0).astype(I32)[:1]
    comb = jnp.concatenate([comb_l[k] for k in range(don_size)], axis=1)
    table = jnp.concatenate(
        [(comb & 1).astype(F32), ((comb >> 1) & 255).astype(F32), (comb >> 9).astype(F32)], axis=0
    ).astype(BF16)
    stage_four(0)
    for n in range(0, rows_live, chunk):
        size = min(chunk, rows_live - n)
        span = slice(n, n + size)
        row = lax.broadcasted_iota(I32, (size, sites), 0) + n
        pick = jnp.where(row == rank_d, 1.0, 0.0).astype(BF16)
        d = jnp.dot(pick, xd[...].reshape(sites, width), preferred_element_type=F32)
        d_s[span, :] = d.astype(BF16)
        tab_s[:, span] = contract_last(table, pick)
    copies[4].wait()

    def project(t):
        for n in range(0, rows_live, chunk):
            span = slice(n, min(n + chunk, rows_live))
            p_s[t, span, :] = jnp.dot(d_s[span, :], w_s[t], preferred_element_type=F32).astype(BF16)

    late = half // 2
    for t in range(late):
        project(t)
    stage_three(1, False)
    for t in range(late, half):
        project(t)
    for n in range(0, rows_d, chunk):
        span = slice(n, n + chunk)
        dt_s[:, span] = jnp.transpose(d_s[span, :].astype(F32)).astype(BF16)

    stage_four(1)
    for n in range(0, rows_live, chunk):
        size = min(chunk, rows_live - n)
        row = lax.broadcasted_iota(I32, (size, sites), 0) + n
        pick = jnp.where(row == rank_s[:1, :], 1.0, 0.0).astype(BF16)
        a_s[n : n + size, :] = jnp.dot(
            pick, xa[...].reshape(sites, width), preferred_element_type=F32
        ).astype(BF16)

    label_col = jnp.transpose(jnp.broadcast_to(label_s[:1, :rows_a].astype(F32), (128, rows_a)))[:rows_live]
    lost = []
    kept = []

    def hits(t, span):
        goal = tab_s[half + t : half + t + 1, span] + 256.0 * tab_s[2 * half + t : 2 * half + t + 1, span]
        return jnp.concatenate([label_col] * (chunk // 128), axis=1) == goal

    deep = e_s.shape[0]

    def score(t):
        for n in range(0, rows_d, chunk):
            span = slice(n, n + chunk)
            raw = contract_last(a_s[:rows_live, :], p_s[t, span, :])
            if rows_live > live:
                row = lax.broadcasted_iota(I32, raw.shape, 0)
                raw = jnp.where(row < live, raw, -1e30)
            weight = tab_s[t : t + 1, span]
            highest = jnp.max(raw, axis=0, keepdims=True)
            expo = jnp.exp2((raw - highest) * (scale * LOG2E))
            e_s[t % deep, :, span] = expo
            summed = jnp.sum(expo, axis=0, keepdims=True)
            picked = jnp.sum(jnp.where(hits(t, span), raw, 0.0), axis=0, keepdims=True)
            lost.append(weight * (jnp.log(summed) + scale * (highest - picked)))
            kept.append((t, span, weight, weight / summed))
    at_loss = core * acc_size + acc
    loss_copies = []

    def send_loss():
        num = sum(jnp.sum(part) for part in lost)
        cnt = sum(jnp.sum(weight) for _, _, weight, _ in kept)
        first_row = lax.broadcasted_iota(I32, loss_s.shape, 0) == 0
        loss_s[...] = jnp.where(first_row, num, cnt)
        for k, peer in enumerate(lossers):
            copy = pltpu.make_async_remote_copy(
                src_ref=loss_s, dst_ref=loss_l.at[at_loss], send_sem=loss_send.at[k], recv_sem=loss_recv.at[k],
                device_id=peer, device_id_type=MESH,
            )
            copy.start()
            loss_copies.append(copy)
        loss_l[at_loss] = loss_s[...]

    tot_copies = []

    def back(t):
        for t_at, span, weight, factor in kept:
            if t_at == t:
                prob = e_s[t % deep, :, span] * factor
                ds_s[t % deep, :rows_live, span] = jnp.where(hits(t, span), prob - weight, prob).astype(BF16)
        at = core * half + t
        for mine in (False, True):
            which = core if mine else 1 - core
            rows = pl.multiple_of((x * 2 + which) * depth, depth)
            total = contract_last(dt_s[pl.ds(rows, depth), :], ds_s[t % deep]) * scale
            if mine:
                tot_out[at] = total.astype(BF16)
            else:
                tot_s[t] = total.astype(BF16)
                copy = pltpu.make_async_remote_copy(
                    src_ref=tot_s.at[t], dst_ref=tot_out.at[at], send_sem=tot_send.at[t], recv_sem=tot_recv.at[t],
                    device_id=sibling, device_id_type=MESH,
                )
                copy.start()
                tot_copies.append(copy)

    for first in range(0, half, deep):
        for t in range(first, first + deep):
            score(t)
        if first + deep == half:
            send_loss()
        for t in range(first, first + deep):
            back(t)

    for copy in loss_copies:
        copy.wait()
    total = loss_l[0]
    for k in range(1, 2 * acc_size):
        total = total + loss_l[k]
    loss_out[...] = jnp.broadcast_to(total[:1] / jnp.maximum(total[1:2], 1.0), loss_out.shape)
    for copy in sent:
        copy.wait_send()
    for copy in tot_copies:
        copy.wait()


def main(don_size, acc_size, dpos, apos, dcnt, acnt, demb, aemb, target, mask, weights):
    slots, width = dpos.shape[0], demb.shape[1]
    tis = weights.shape[0]
    half = tis // 2
    shards = don_size * acc_size
    sites = shards * slots
    live = shards * (slots + 1) // 2
    padded = round_up(live, 128)
    depth = width // don_size
    inner = 1
    while (2 * inner) ** 2 <= acc_size:
        inner *= 2
    outer, chips = acc_size // inner, don_size // 2
    same = shards // 2
    sends = (outer - 1) + outer * (inner - 1) + outer * inner * (chips - 1) + same
    tile_rows = max(8, tis)
    hbm = pl.BlockSpec(memory_space=pltpu.HBM)
    vmem = pl.BlockSpec(memory_space=pltpu.VMEM)
    dma = pltpu.SemaphoreType.DMA
    lossers = 2 * acc_size - 1
    deep = half if half * padded * padded <= 1 << 21 else 1
    arrays = 2 * width * (2 * demb.shape[0] + half * width + 3 * sites + (3 + half) * padded + tis * depth)
    limit = arrays + arrays // 4 + deep * padded * padded * 6 + (8 << 20)
    return pl.pallas_call(
        functools.partial(main_kernel, don_size, acc_size, inner, live),
        in_specs=[hbm] * 9,
        out_specs=[vmem, vmem, vmem],
        out_shape=[
            jax.ShapeDtypeStruct((tis, depth, padded), BF16),
            jax.ShapeDtypeStruct((padded, width), BF16),
            jax.ShapeDtypeStruct((8, 128), F32),
        ],
        scratch_shapes=[
            pltpu.SMEM(dpos.shape, I32),
            pltpu.SMEM(apos.shape, I32),
            pltpu.SMEM(dcnt.shape, I32),
            pltpu.SMEM(acnt.shape, I32),
            pltpu.VMEM(demb.shape, BF16),
            pltpu.VMEM(aemb.shape, BF16),
            pltpu.VMEM((half, width, width), BF16),
            pltpu.VMEM((2, tile_rows, sites // don_size), I32),
            pltpu.VMEM((shards, slots, width), BF16),
            pltpu.VMEM((shards, slots, width), BF16),
            pltpu.VMEM((2, half, sites // don_size), I32),
            pltpu.VMEM((don_size, half, sites // don_size), I32),
            pltpu.VMEM((8, 128), F32),
            pltpu.VMEM((don_size, 8, 128), F32),
            pltpu.VMEM((padded, width), BF16),
            pltpu.VMEM((width, padded), BF16),
            pltpu.VMEM((half, padded, width), BF16),
            pltpu.VMEM((deep, round_up(live, 16), padded), F32),
            pltpu.VMEM((deep, padded, padded), BF16),
            pltpu.VMEM((half, depth, padded), BF16),
            pltpu.VMEM((8, sites), I32),
            pltpu.VMEM((8, sites), I32),
            pltpu.VMEM((3 * half, padded), F32),
            pltpu.VMEM((2, 128, sites), BF16),
            pltpu.VMEM((8, 128), F32),
            pltpu.VMEM((2 * acc_size, 8, 128), F32),
            dma((9,)),
            dma((2, sends)),
            dma((2, shards)),
            dma((1,)),
            dma((1,)),
            dma((don_size - 1, 2)),
            dma((don_size - 1, 2)),
            dma((half,)),
            dma((half,)),
            dma((lossers,)),
            dma((lossers,)),
        ],
        compiler_params=pltpu.CompilerParams(
            collective_id=0, has_side_effects=True, vmem_limit_bytes=min(limit, 60 << 20)
        ),
    )(*[
        pltpu.with_memory_space_constraint(array, pltpu.HBM)
        for array in (dpos, apos, dcnt, acnt, demb, aemb, target, mask, weights)
    ])


def grad_kernel(tot_ref, a_ref, loss_ref, grad_ref, out_ref, buf, sem):
    copies = []
    for t in range(tot_ref.shape[0]):
        buf[t] = jnp.dot(tot_ref[t], a_ref[...], preferred_element_type=F32)
        copy = pltpu.make_async_copy(buf.at[t], grad_ref.at[:, t, :], sem.at[t])
        copy.start()
        copies.append(copy)
    out_ref[0, 0] = jnp.max(loss_ref[...])
    for copy in copies:
        copy.wait()


def grad(total, a, loss):
    tis, depth, _ = total.shape
    width = a.shape[1]
    vmem = pl.BlockSpec(memory_space=pltpu.VMEM)
    return pl.pallas_call(
        grad_kernel,
        in_specs=[vmem, vmem, vmem],
        out_specs=[pl.BlockSpec(memory_space=pl.ANY), pl.BlockSpec(memory_space=pltpu.SMEM)],
        out_shape=[jax.ShapeDtypeStruct((depth, tis, width), F32), jax.ShapeDtypeStruct((1, 1), F32)],
        scratch_shapes=[pltpu.VMEM((tis, depth, width), F32), pltpu.SemaphoreType.DMA((tis,))],
        compiler_params=pltpu.CompilerParams(vmem_limit_bytes=round_up(2 * tis * depth * width * 4, 1 << 20)),
    )(total, a, loss)


def local(
    don_size, acc_size, donor_emb, acceptor_emb, donor_pos, acceptor_pos, donor_count, acceptor_count,
    target, junction_mask, weights,
):
    total, a, loss = main(
        don_size, acc_size, donor_pos, acceptor_pos, donor_count, acceptor_count,
        donor_emb, acceptor_emb, target, junction_mask, weights,
    )
    grad_weight, loss = grad(total, a, loss)
    return loss.reshape(()), grad_weight


def solution(mesh):
    return jax.shard_map(
        functools.partial(local, mesh.shape["don"], mesh.shape["acc"]),
        mesh=mesh,
        in_specs=(
            P(("don", "acc"), None),
            P(("don", "acc"), None),
            P(("don", "acc")),
            P(("don", "acc")),
            P("don"),
            P(),
            P(None, "don"),
            P(None, "don"),
            P("acc", None, None),
        ),
        out_specs=(P(), P("don", "acc", None)),
        check_vma=False,
    )
```

```python
import functools
import itertools

import jax
import jax.numpy as jnp
from jax import lax
from jax.experimental import pallas as pl
from jax.experimental.pallas import tpu as pltpu
from jax.sharding import PartitionSpec as P

BF16 = jnp.bfloat16
F32 = jnp.float32
I32 = jnp.int32
MESH = pl.DeviceIdType.MESH
DIRECT = 9
PIECES = 4
LOG2E = 1.4426950408889634


def round_up(n, m):
    return (n + m - 1) // m * m


def row_chunk(n, limit=512):
    best = 128
    for r in range(128, limit + 1, 128):
        if n % r == 0:
            best = r
    return best


def contract_last(a, b):
    return lax.dot_general(a, b, (((1,), (1,)), ((), ())), preferred_element_type=F32)


def acceptor_tables(counts, shards, slots, width):
    col = lax.broadcasted_iota(I32, (8, width), 1)

    def step(k, carry):
        first, rank, label = carry
        number = counts[k]
        within = col - k * slots
        live = (within >= 0) & (within < number)
        rank = jnp.where(live, first + within, rank)
        last = first + number
        return last, rank, label + jnp.where(col >= last, slots - number, 0)

    return lax.fori_loop(0, shards, step, (jnp.int32(0), jnp.full((8, width), -1, I32), col))[1:]


def main_kernel(
    don_size, acc_size, inner, live,
    dpos_h, apos_h, dcnt_h, acnt_h, demb, aemb, target, mask, weights,
    grad_out, loss_out,
    dpos, apos, dcnt, acnt, demb_v, aemb_v, w_s, tm_s, xd, xa, comb_s, comb_l, cnt_s, cnt_l,
    d_s, dt_s, a_s, p_s, e_s, ds_s, tot_out, tot_s, rank_s, label_s, tab_s, first_s, loss_s, loss_l,
    in_sem, row_sem, send_sem, recv_sem, sib_send, sib_recv, side_send, side_recv,
    tot_send, tot_recv, loss_send, loss_recv,
):
    shards, slots, width = xd.shape
    outer, chips = acc_size // inner, don_size // 2
    sites = shards * slots
    don_sites = sites // don_size
    half, rows_d = w_s.shape[0], d_s.shape[0]
    rows_a = a_s.shape[0]
    depth = width // don_size
    tis = 2 * half
    scale = width ** (-0.5)
    alternate = chips == inner
    don, acc = lax.axis_index("don"), lax.axis_index("acc")
    core, x = lax.rem(don, 2), don // 2
    o, i = acc // inner, lax.rem(acc, inner)
    if alternate:
        b = core * x + (1 - core) * i
        c = core * i + (1 - core) * x
        b_size, c_size = inner, inner
    else:
        b, c, b_size, c_size = i, x, inner, chips

    def place(oo, bb, cc):
        if alternate:
            xx = core * bb + (1 - core) * cc
            ii = core * cc + (1 - core) * bb
        else:
            xx, ii = cc, bb
        return (xx * 2 + core, oo * inner + ii)

    def away(at, k, size):
        return lax.rem(at + k, size)

    def near(at, k, size):
        up = k - 1 + jnp.where(k - 1 >= at, 1, 0)
        down = k - 1 + jnp.where(k - 1 >= size - 1 - at, 1, 0)
        return jnp.where(2 * at < size, up, size - 1 - down)

    def slot_of(at):
        return at[0] * acc_size + at[1]

    sibling = (x * 2 + 1 - core, acc)

    tile_rows = tm_s.shape[1]
    row_at = pl.multiple_of(acc * tis // tile_rows * tile_rows, tile_rows)
    copies = [
        None,
        pltpu.make_async_copy(target.at[pl.ds(row_at, tile_rows), :], tm_s.at[0], in_sem.at[1]),
        pltpu.make_async_copy(mask.at[pl.ds(row_at, tile_rows), :], tm_s.at[1], in_sem.at[2]),
        None,
        pltpu.make_async_copy(weights.at[pl.ds(core * half, half)], w_s, in_sem.at[4]),
    ]
    small = [
        pltpu.make_async_copy(source, dest, in_sem.at[5 + k])
        for k, (source, dest) in enumerate(((dpos_h, dpos), (apos_h, apos), (dcnt_h, dcnt), (acnt_h, acnt)))
    ]
    piece = demb_v.shape[0] // PIECES
    rows_in = [
        [
            pltpu.make_async_copy(
                emb.at[pl.ds(n * piece, piece), :], emb_v.at[pl.ds(n * piece, piece), :], row_sem.at[which, n]
            )
            for n in range(PIECES)
        ]
        for which, (emb, emb_v) in enumerate(((demb, demb_v), (aemb, aemb_v)))
    ]
    for copy in small[:2] + rows_in[0] + small[2:] + copies[1:3] + rows_in[1]:
        copy.start()

    others = [(away(don, k, don_size), acc) for k in range(1, don_size)]
    lossers = [
        (x * 2 + away(core, kc, 2), away(acc, ka, acc_size))
        for kc in range(2) for ka in range(acc_size) if kc or ka
    ]
    far = [
        (away(x, k, chips) * 2 + kc, acc) for k in range(1, chips) for kc in range(2)
    ]
    corner = [
        place(o, away(b, kb, b_size), away(c, kc, c_size)) for kb in range(1, b_size) for kc in range(1, c_size)
    ]
    barrier = pltpu.get_barrier_semaphore()
    for peer in lossers + far + corner:
        pl.semaphore_signal(barrier, inc=1, device_id=peer, device_id_type=MESH)

    def own_rows(pos, which, landing):
        emb_v = (demb_v, aemb_v)[which]
        small[which].wait()
        row = lax.broadcasted_iota(I32, (slots, 128), 0)
        want = jnp.zeros((slots, 128), I32)
        for k in range(slots):
            want = jnp.where(row == k, pos[k], want)
        col = lax.broadcasted_iota(I32, (slots, piece), 1)
        want = jnp.concatenate([want] * (piece // 128), axis=1)
        rows = jnp.zeros((slots, width), F32)
        for n in range(PIECES):
            pick = jnp.where(col + n * piece == want, 1.0, 0.0).astype(BF16)
            rows_in[which][n].wait()
            rows = rows + jnp.dot(pick, emb_v[n * piece : (n + 1) * piece, :], preferred_element_type=F32)
        landing[held] = rows.astype(BF16)

    held = don * acc_size + acc
    own_rows(dpos, 0, xd)
    pl.semaphore_wait(barrier, len(lossers) + len(far) + len(corner))

    sent = []
    land = (xd, xa)

    def send(kind, source, slot, peer, count):
        n = count[kind]
        count[kind] += 1
        copy = pltpu.make_async_remote_copy(
            src_ref=source, dst_ref=land[kind].at[slot],
            send_sem=send_sem.at[kind, n], recv_sem=recv_sem.at[kind, slot],
            device_id=peer, device_id_type=MESH,
        )
        copy.start()
        sent.append(copy)

    def arrived(kind, slot):
        pltpu.make_async_copy(land[kind].at[slot], land[kind].at[slot], recv_sem.at[kind, slot]).wait()

    counter = [0, 0]

    def at_offset(ko, kb, kc):
        return place(near(o, ko, outer) if ko else o, away(b, kb, b_size), away(c, kc, c_size))

    def targets(ko, kb, kc):
        along_b = [(0, k, 0) for k in range(1, b_size)]
        along_c = [(0, 0, k) for k in range(1, c_size)]
        both = [(0, k, m) for k in range(1, b_size) for m in range(1, c_size)]
        if kc or (kb and ko >= DIRECT):
            return []
        if kb:
            return along_c
        if ko >= DIRECT:
            return both + along_b + along_c
        return ([] if ko else [(k, 0, 0) for k in range(outer - 1, 0, -1)]) + along_b + along_c

    def forward(kind, offset):
        slot = slot_of(at_offset(*offset))
        for hop in targets(*offset):
            send(kind, land[kind].at[slot], slot, at_offset(*hop), counter)
        send(kind, land[kind].at[slot], slot, sibling, counter)

    def relay(kind, offset):
        arrived(kind, slot_of(at_offset(*offset)))
        forward(kind, offset)

    every = list(itertools.product(range(outer), range(b_size), range(c_size)))

    def relays(kind, b_far, c_far):
        for ko, kb, kc in every:
            if (ko or kb or kc) and (kb > 0) == b_far and (kc > 0) == c_far:
                relay(kind, (ko, kb, kc))

    def relays_one(kind):
        for kb in range(1, b_size):
            relay(kind, (0, kb, 0))
        relays(kind, False, False)

    def relays_two(kind):
        for ko in range(1, outer):
            for kb in range(1, b_size):
                relay(kind, (ko, kb, 0))

    forward(0, (0, 0, 0))
    own_rows(apos, 1, xa)
    forward(1, (0, 0, 0))
    copies[4].start()
    copies[1].wait()
    copies[2].wait()
    both = tm_s[0] * 2 + tm_s[1]
    for core_at in range(2):
        mine = both[core_at * half : (core_at + 1) * half]
        for k in range(1, tile_rows // tis):
            at = k * tis + core_at * half
            mine = jnp.where(lax.rem(acc, tile_rows // tis) == k, both[at : at + half], mine)
        comb_s[core_at] = mine

    for copy in small[2:]:
        copy.wait()
    lane = lax.broadcasted_iota(I32, (1, 128), 1)
    counts = jnp.zeros((1, 128), F32)
    for k in range(shards // don_size):
        counts = jnp.where(lane == don * (shards // don_size) + k, dcnt[k].astype(F32), counts)
    cnt_s[...] = jnp.broadcast_to(counts, cnt_s.shape)
    side = []
    for k, peer in enumerate(others):
        to = lax.rem(peer[0], 2)
        for j, (source, dest) in enumerate(((comb_s.at[to], comb_l.at[don]), (cnt_s, cnt_l.at[don]))):
            copy = pltpu.make_async_remote_copy(
                src_ref=source, dst_ref=dest, send_sem=side_send.at[k, j], recv_sem=side_recv.at[k, j],
                device_id=peer, device_id_type=MESH,
            )
            copy.start()
            side.append(copy)
    comb_l[don] = comb_s[core]
    cnt_l[don] = cnt_s[...]

    rank_a, label_a = acceptor_tables(acnt, shards, slots, sites)
    rank_s[...] = rank_a
    label_s[...] = label_a
    shard_row = lax.broadcasted_iota(I32, (first_s.shape[1], sites), 0)
    slot_lane = lax.broadcasted_iota(I32, (first_s.shape[1], sites), 1)
    before = slot_lane >= (shard_row + 1) * slots
    within_shard = (slot_lane >= shard_row * slots) & jnp.logical_not(before)
    first_s[0] = jnp.where(before, 1.0, 0.0).astype(BF16)
    first_s[1] = jnp.where(within_shard, 1.0, 0.0).astype(BF16)

    rows_live = round_up(live, 16)
    chunk = row_chunk(rows_d)
    if rows_a > rows_live:
        a_s[rows_live:, :] = jnp.zeros((rows_a - rows_live, width), BF16)
        d_s[rows_live:, :] = jnp.zeros((rows_d - rows_live, width), BF16)
        tab_s[:, rows_live:] = jnp.zeros((tab_s.shape[0], rows_d - rows_live), F32)
        for t in range(half):
            p_s[t, rows_live:, :] = jnp.zeros((rows_d - rows_live, width), BF16)
        for t in range(ds_s.shape[0]):
            ds_s[t, rows_live:, :] = jnp.zeros((rows_a - rows_live, rows_d), BF16)


    def stage_four(kind):
        for kx in range(chips):
            for ka in range(acc_size):
                arrived(kind, slot_of((away(x, kx, chips) * 2 + 1 - core, away(acc, ka, acc_size))))

    relays_one(0)
    relays_one(1)
    relays_two(0)
    relays(0, False, True)
    relays_two(1)
    relays(0, True, True)
    relays(1, False, True)

    for copy in side:
        copy.wait()
    counts = cnt_l[0]
    for k in range(1, don_size):
        counts = counts + cnt_l[k]
    counts = counts.astype(BF16)
    first = jnp.dot(counts, first_s[0], preferred_element_type=F32)
    number = jnp.dot(counts, first_s[1], preferred_element_type=F32)
    shard_of = jnp.sum(first_s[0].astype(F32), axis=0, keepdims=True)
    within = lax.broadcasted_iota(I32, (8, sites), 1).astype(F32) - shard_of * slots
    rank_d = jnp.where(within < number, first + within, -1.0).astype(I32)[:1]
    comb = jnp.concatenate([comb_l[k] for k in range(don_size)], axis=1)
    table = jnp.concatenate(
        [(comb & 1).astype(F32), ((comb >> 1) & 255).astype(F32), (comb >> 9).astype(F32)], axis=0
    ).astype(BF16)
    stage_four(0)
    for n in range(0, rows_live, chunk):
        size = min(chunk, rows_live - n)
        span = slice(n, n + size)
        row = lax.broadcasted_iota(I32, (size, sites), 0) + n
        pick = jnp.where(row == rank_d, 1.0, 0.0).astype(BF16)
        d = jnp.dot(pick, xd[...].reshape(sites, width), preferred_element_type=F32)
        d_s[span, :] = d.astype(BF16)
        tab_s[:, span] = contract_last(table, pick)
    copies[4].wait()

    def project(t):
        for n in range(0, rows_live, chunk):
            span = slice(n, min(n + chunk, rows_live))
            p_s[t, span, :] = jnp.dot(d_s[span, :], w_s[t], preferred_element_type=F32).astype(BF16)

    for t in range(half):
        if t == half // 2:
            relays(1, True, True)
        project(t)
    for n in range(0, rows_d, chunk):
        span = slice(n, n + chunk)
        dt_s[:, span] = jnp.transpose(d_s[span, :].astype(F32)).astype(BF16)

    stage_four(1)
    for n in range(0, rows_live, chunk):
        size = min(chunk, rows_live - n)
        row = lax.broadcasted_iota(I32, (size, sites), 0) + n
        pick = jnp.where(row == rank_s[:1, :], 1.0, 0.0).astype(BF16)
        a_s[n : n + size, :] = jnp.dot(
            pick, xa[...].reshape(sites, width), preferred_element_type=F32
        ).astype(BF16)

    label_col = jnp.transpose(jnp.broadcast_to(label_s[:1, :rows_a].astype(F32), (128, rows_a)))[:rows_live]
    lost = []
    kept = []

    def hits(t, span):
        goal = tab_s[half + t : half + t + 1, span] + 256.0 * tab_s[2 * half + t : 2 * half + t + 1, span]
        return jnp.concatenate([label_col] * (chunk // 128), axis=1) == goal

    deep = e_s.shape[0]

    def score(t):
        for n in range(0, rows_d, chunk):
            span = slice(n, n + chunk)
            raw = contract_last(a_s[:rows_live, :], p_s[t, span, :])
            if rows_live > live:
                row = lax.broadcasted_iota(I32, raw.shape, 0)
                raw = jnp.where(row < live, raw, -1e30)
            weight = tab_s[t : t + 1, span]
            highest = jnp.max(raw, axis=0, keepdims=True)
            expo = jnp.exp2((raw - highest) * (scale * LOG2E))
            e_s[t % deep, :, span] = expo
            summed = jnp.sum(expo, axis=0, keepdims=True)
            picked = jnp.sum(jnp.where(hits(t, span), raw, 0.0), axis=0, keepdims=True)
            lost.append(weight * (jnp.log(summed) + scale * (highest - picked)))
            kept.append((t, span, weight, weight / summed))
    at_loss = core * acc_size + acc
    loss_copies = []

    def send_loss():
        num = sum(jnp.sum(part) for part in lost)
        cnt = sum(jnp.sum(weight) for _, _, weight, _ in kept)
        first_row = lax.broadcasted_iota(I32, loss_s.shape, 0) == 0
        loss_s[...] = jnp.where(first_row, num, cnt)
        for k, peer in enumerate(lossers):
            copy = pltpu.make_async_remote_copy(
                src_ref=loss_s, dst_ref=loss_l.at[at_loss], send_sem=loss_send.at[k], recv_sem=loss_recv.at[k],
                device_id=peer, device_id_type=MESH,
            )
            copy.start()
            loss_copies.append(copy)
        loss_l[at_loss] = loss_s[...]

    tot_copies = []

    def back(t):
        for t_at, span, weight, factor in kept:
            if t_at == t:
                prob = e_s[t % deep, :, span] * factor
                ds_s[t % deep, :rows_live, span] = jnp.where(hits(t, span), prob - weight, prob).astype(BF16)
        at = core * half + t
        for mine in (False, True):
            which = core if mine else 1 - core
            rows = pl.multiple_of((x * 2 + which) * depth, depth)
            total = contract_last(dt_s[pl.ds(rows, depth), :], ds_s[t % deep]) * scale
            if mine:
                tot_out[at] = total.astype(BF16)
            else:
                tot_s[t] = total.astype(BF16)
                copy = pltpu.make_async_remote_copy(
                    src_ref=tot_s.at[t], dst_ref=tot_out.at[at], send_sem=tot_send.at[t], recv_sem=tot_recv.at[t],
                    device_id=sibling, device_id_type=MESH,
                )
                copy.start()
                tot_copies.append(copy)

    for first in range(0, half, deep):
        for t in range(first, first + deep):
            score(t)
        if first + deep == half:
            send_loss()
        for t in range(first, first + deep):
            back(t)

    def gradient(at):
        grad_out[at] = jnp.dot(tot_out[at], a_s[...], preferred_element_type=F32)

    for t in range(half):
        gradient(core * half + t)
    for t in range(half):
        tot_copies[t].wait()
        gradient((1 - core) * half + t)
    for copy in loss_copies:
        copy.wait()
    total = loss_l[0]
    for k in range(1, 2 * acc_size):
        total = total + loss_l[k]
    loss_out[...] = jnp.broadcast_to(total[:1] / jnp.maximum(total[1:2], 1.0), loss_out.shape)
    for copy in sent:
        copy.wait_send()


def main(don_size, acc_size, dpos, apos, dcnt, acnt, demb, aemb, target, mask, weights):
    slots, width = dpos.shape[0], demb.shape[1]
    tis = weights.shape[0]
    half = tis // 2
    shards = don_size * acc_size
    sites = shards * slots
    live = shards * (slots + 1) // 2
    padded = round_up(live, 128)
    depth = width // don_size
    inner = 1
    while (2 * inner) ** 2 <= acc_size:
        inner *= 2
    outer, chips = acc_size // inner, don_size // 2
    sends = shards // 2 + (outer - 1) + outer * inner * chips - outer
    tile_rows = max(8, tis)
    hbm = pl.BlockSpec(memory_space=pltpu.HBM)
    vmem = pl.BlockSpec(memory_space=pltpu.VMEM)
    dma = pltpu.SemaphoreType.DMA
    lossers = 2 * acc_size - 1
    deep = half if half * padded * padded <= 1 << 21 else 1
    arrays = 2 * width * (2 * demb.shape[0] + half * width + 3 * sites + (3 + half) * padded + tis * depth)
    limit = arrays + arrays // 4 + deep * padded * padded * 6 + (8 << 20)
    return pl.pallas_call(
        functools.partial(main_kernel, don_size, acc_size, inner, live),
        in_specs=[hbm] * 9,
        out_specs=[vmem, vmem],
        out_shape=[
            jax.ShapeDtypeStruct((tis, depth, width), F32),
            jax.ShapeDtypeStruct((8, 128), F32),
        ],
        scratch_shapes=[
            pltpu.SMEM(dpos.shape, I32),
            pltpu.SMEM(apos.shape, I32),
            pltpu.SMEM(dcnt.shape, I32),
            pltpu.SMEM(acnt.shape, I32),
            pltpu.VMEM(demb.shape, BF16),
            pltpu.VMEM(aemb.shape, BF16),
            pltpu.VMEM((half, width, width), BF16),
            pltpu.VMEM((2, tile_rows, sites // don_size), I32),
            pltpu.VMEM((shards, slots, width), BF16),
            pltpu.VMEM((shards, slots, width), BF16),
            pltpu.VMEM((2, half, sites // don_size), I32),
            pltpu.VMEM((don_size, half, sites // don_size), I32),
            pltpu.VMEM((8, 128), F32),
            pltpu.VMEM((don_size, 8, 128), F32),
            pltpu.VMEM((padded, width), BF16),
            pltpu.VMEM((width, padded), BF16),
            pltpu.VMEM((padded, width), BF16),
            pltpu.VMEM((half, padded, width), BF16),
            pltpu.VMEM((deep, round_up(live, 16), padded), F32),
            pltpu.VMEM((deep, padded, padded), BF16),
            pltpu.VMEM((tis, depth, padded), BF16),
            pltpu.VMEM((half, depth, padded), BF16),
            pltpu.VMEM((8, sites), I32),
            pltpu.VMEM((8, sites), I32),
            pltpu.VMEM((3 * half, padded), F32),
            pltpu.VMEM((2, 128, sites), BF16),
            pltpu.VMEM((8, 128), F32),
            pltpu.VMEM((2 * acc_size, 8, 128), F32),
            dma((9,)),
            dma((2, PIECES)),
            dma((2, sends)),
            dma((2, shards)),
            dma((1,)),
            dma((1,)),
            dma((don_size - 1, 2)),
            dma((don_size - 1, 2)),
            dma((half,)),
            dma((half,)),
            dma((lossers,)),
            dma((lossers,)),
        ],
        compiler_params=pltpu.CompilerParams(
            collective_id=0, has_side_effects=True, vmem_limit_bytes=min(limit, 60 << 20)
        ),
    )(*[
        pltpu.with_memory_space_constraint(array, pltpu.HBM)
        for array in (dpos, apos, dcnt, acnt, demb, aemb, target, mask, weights)
    ])


def grad_kernel(buf, loss_ref, grad_ref, out_ref, sem):
    copies = []
    for t in range(buf.shape[0]):
        copy = pltpu.make_async_copy(buf.at[t], grad_ref.at[:, t, :], sem.at[t])
        copy.start()
        copies.append(copy)
    out_ref[0, 0] = jnp.max(loss_ref[...])
    for copy in copies:
        copy.wait()


def grad(by_tissue, loss):
    tis, depth, width = by_tissue.shape
    vmem = pl.BlockSpec(memory_space=pltpu.VMEM)
    return pl.pallas_call(
        grad_kernel,
        in_specs=[vmem, vmem],
        out_specs=[pl.BlockSpec(memory_space=pl.ANY), pl.BlockSpec(memory_space=pltpu.SMEM)],
        out_shape=[jax.ShapeDtypeStruct((depth, tis, width), F32), jax.ShapeDtypeStruct((1, 1), F32)],
        scratch_shapes=[pltpu.SemaphoreType.DMA((tis,))],
        compiler_params=pltpu.CompilerParams(vmem_limit_bytes=8 << 20),
    )(by_tissue, loss)


def local(
    don_size, acc_size, donor_emb, acceptor_emb, donor_pos, acceptor_pos, donor_count, acceptor_count,
    target, junction_mask, weights,
):
    by_tissue, loss = main(
        don_size, acc_size, donor_pos, acceptor_pos, donor_count, acceptor_count,
        donor_emb, acceptor_emb, target, junction_mask, weights,
    )
    grad_weight, loss = grad(by_tissue, loss)
    return loss.reshape(()), grad_weight


def solution(mesh):
    return jax.shard_map(
        functools.partial(local, mesh.shape["don"], mesh.shape["acc"]),
        mesh=mesh,
        in_specs=(
            P(("don", "acc"), None),
            P(("don", "acc"), None),
            P(("don", "acc")),
            P(("don", "acc")),
            P("don"),
            P(),
            P(None, "don"),
            P(None, "don"),
            P("acc", None, None),
        ),
        out_specs=(P(), P("don", "acc", None)),
        check_vma=False,
    )
```

```python
import functools
import itertools
import math

import jax
import jax.numpy as jnp
from jax import lax
from jax.experimental import pallas as pl
from jax.experimental.pallas import tpu as pltpu
from jax.sharding import PartitionSpec as P

BF16 = jnp.bfloat16
F32 = jnp.float32
I32 = jnp.int32
MESH = pl.DeviceIdType.MESH
PIECES = 4
LOG2E = 1.4426950408889634


def round_up(n, m):
    return (n + m - 1) // m * m


def row_chunk(n, limit=512):
    best = 128
    for r in range(128, limit + 1, 128):
        if n % r == 0:
            best = r
    return best


def contract_last(a, b):
    return lax.dot_general(a, b, (((1,), (1,)), ((), ())), preferred_element_type=F32)


def acceptor_tables(counts, shards, slots, width):
    col = lax.broadcasted_iota(I32, (8, width), 1)

    def step(k, carry):
        first, rank, label = carry
        number = counts[k]
        within = col - k * slots
        live = (within >= 0) & (within < number)
        rank = jnp.where(live, first + within, rank)
        last = first + number
        return last, rank, label + jnp.where(col >= last, slots - number, 0)

    return lax.fori_loop(0, shards, step, (jnp.int32(0), jnp.full((8, width), -1, I32), col))[1:]


def main_kernel(
    don_size, acc_size, inner, live,
    dpos_h, apos_h, dcnt_h, acnt_h, demb, aemb, target, mask, weights,
    grad_out, loss_out,
    dpos, apos, dcnt, acnt, demb_v, aemb_v, w_s, tm_s, xd, xa, comb_s, comb_l, cnt_s, cnt_l,
    d_s, dt_s, a_s, p_s, e_s, ds_s, tot_out, tot_s, rank_s, label_s, tab_s, first_s, loss_s, loss_l,
    in_sem, w_sem, row_sem, send_sem, recv_sem, sib_send, sib_recv, side_send, side_recv,
    tot_send, tot_recv, loss_send, loss_recv,
):
    shards, slots, width = xd.shape
    outer, chips = acc_size // inner, don_size // 2
    sites = shards * slots
    don_sites = sites // don_size
    half, rows_d = w_s.shape[0], d_s.shape[0]
    rows_a = a_s.shape[0]
    depth = width // don_size
    tis = 2 * half
    scale = width ** (-0.5)
    alternate = chips == inner
    don, acc = lax.axis_index("don"), lax.axis_index("acc")
    core, x = lax.rem(don, 2), don // 2
    o, i = acc // inner, lax.rem(acc, inner)
    if alternate:
        b = core * x + (1 - core) * i
        c = core * i + (1 - core) * x
        b_size, c_size = inner, inner
    else:
        b, c, b_size, c_size = i, x, inner, chips

    def place(oo, bb, cc):
        if alternate:
            xx = core * bb + (1 - core) * cc
            ii = core * cc + (1 - core) * bb
        else:
            xx, ii = cc, bb
        return (xx * 2 + core, oo * inner + ii)

    def away(at, k, size):
        return lax.rem(at + k, size)

    def near(at, k, size):
        up = k - 1 + jnp.where(k - 1 >= at, 1, 0)
        down = k - 1 + jnp.where(k - 1 >= size - 1 - at, 1, 0)
        return jnp.where(2 * at < size, up, size - 1 - down)

    def slot_of(at):
        return at[0] * acc_size + at[1]

    sibling = (x * 2 + 1 - core, acc)
    parts = 1
    share = half // parts

    def tissue(k):
        return k

    tile_rows = tm_s.shape[1]
    row_at = pl.multiple_of(acc * tis // tile_rows * tile_rows, tile_rows)
    copies = [
        None,
        pltpu.make_async_copy(target.at[pl.ds(row_at, tile_rows), :], tm_s.at[0], in_sem.at[1]),
        pltpu.make_async_copy(mask.at[pl.ds(row_at, tile_rows), :], tm_s.at[1], in_sem.at[2]),
        None,
        None,
    ]
    weights_in = [pltpu.make_async_copy(weights.at[pl.ds(core * half, half)], w_s, w_sem.at[0])]
    small = [
        pltpu.make_async_copy(source, dest, in_sem.at[5 + k])
        for k, (source, dest) in enumerate(((dpos_h, dpos), (apos_h, apos), (dcnt_h, dcnt), (acnt_h, acnt)))
    ]
    piece = demb_v.shape[0] // PIECES
    rows_in = [
        [
            pltpu.make_async_copy(
                emb.at[pl.ds(n * piece, piece), :], emb_v.at[pl.ds(n * piece, piece), :], row_sem.at[which, n]
            )
            for n in range(PIECES)
        ]
        for which, (emb, emb_v) in enumerate(((demb, demb_v), (aemb, aemb_v)))
    ]
    for copy in small[:2] + rows_in[0] + small[2:] + copies[1:3] + rows_in[1]:
        copy.start()

    others = [(away(don, k, don_size), acc) for k in range(1, don_size)]
    lossers = [
        ((x // parts * parts + away(lax.rem(x, parts), kx, parts)) * 2 + away(core, kc, 2), away(acc, ka, acc_size))
        for kx in range(parts) for kc in range(2) for ka in range(acc_size) if kx or kc or ka
    ]
    direct = others + [(don, away(o, k, outer) * inner + i) for k in range(1, outer)]
    direct += [(don, o * inner + away(i, k, inner)) for k in range(1, inner)]
    barrier = pltpu.get_barrier_semaphore()
    for peer in direct:
        pl.semaphore_signal(barrier, inc=1, device_id=peer, device_id_type=MESH)

    def own_rows(pos, which, landing):
        emb_v = (demb_v, aemb_v)[which]
        small[which].wait()
        row = lax.broadcasted_iota(I32, (slots, 128), 0)
        want = jnp.zeros((slots, 128), I32)
        for k in range(slots):
            want = jnp.where(row == k, pos[k], want)
        col = lax.broadcasted_iota(I32, (slots, piece), 1)
        want = jnp.concatenate([want] * (piece // 128), axis=1)
        rows = jnp.zeros((slots, width), F32)
        for n in range(PIECES):
            pick = jnp.where(col + n * piece == want, 1.0, 0.0).astype(BF16)
            rows_in[which][n].wait()
            rows = rows + jnp.dot(pick, emb_v[n * piece : (n + 1) * piece, :], preferred_element_type=F32)
        landing[held] = rows.astype(BF16)

    held = don * acc_size + acc
    own_rows(dpos, 0, xd)
    pl.semaphore_wait(barrier, len(direct))

    sent = []
    land = (xd, xa)

    def send(kind, source, slot, peer, count):
        n = count[kind]
        count[kind] += 1
        copy = pltpu.make_async_remote_copy(
            src_ref=source, dst_ref=land[kind].at[slot],
            send_sem=send_sem.at[kind, n], recv_sem=recv_sem.at[kind, slot],
            device_id=peer, device_id_type=MESH,
        )
        copy.start()
        sent.append(copy)

    def arrived(kind, slot):
        pltpu.make_async_copy(land[kind].at[slot], land[kind].at[slot], recv_sem.at[kind, slot]).wait()

    counter = [0, 0]

    def at_offset(ko, kb, kc):
        return place(near(o, ko, outer) if ko else o, away(b, kb, b_size), away(c, kc, c_size))

    def targets(ko, kb, kc):
        line = [(k, 0, 0) for k in range(outer - 1, 0, -1)]
        along_b = [(0, k, 0) for k in range(1, b_size)]
        along_c = [(0, 0, k) for k in range(1, c_size)]
        return [] if kc else along_c if kb else along_b + along_c if ko else line + along_b + along_c

    def forward(kind, offset):
        slot = slot_of(at_offset(*offset))
        for hop in targets(*offset):
            send(kind, land[kind].at[slot], slot, at_offset(*hop), counter)
        send(kind, land[kind].at[slot], slot, sibling, counter)

    def relay(kind, offset):
        arrived(kind, slot_of(at_offset(*offset)))
        forward(kind, offset)

    every = list(itertools.product(range(outer), range(b_size), range(c_size)))
    relayed = set()

    def relays(kind, chosen):
        for offset in every:
            if any(offset) and chosen(*offset) and (kind, offset) not in relayed:
                relayed.add((kind, offset))
                relay(kind, offset)

    def relays_one(kind):
        relays(kind, lambda ko, kb, kc: not ko and not kc)
        relays(kind, lambda ko, kb, kc: not kb and not kc)

    def relays_two(kind):
        relays(kind, lambda ko, kb, kc: ko and not kc)

    def relays_three(kind):
        relays(kind, lambda ko, kb, kc: not kb)

    def relays_four(kind):
        relays(kind, lambda ko, kb, kc: True)

    forward(0, (0, 0, 0))
    own_rows(apos, 1, xa)
    forward(1, (0, 0, 0))
    for copy in weights_in:
        copy.start()
    copies[1].wait()
    copies[2].wait()
    both = tm_s[0] * 2 + tm_s[1]
    for core_at in range(2):
        mine = both[core_at * half : (core_at + 1) * half]
        for k in range(1, tile_rows // tis):
            at = k * tis + core_at * half
            mine = jnp.where(lax.rem(acc, tile_rows // tis) == k, both[at : at + half], mine)
        comb_s[core_at] = mine

    for copy in small[2:]:
        copy.wait()
    lane = lax.broadcasted_iota(I32, (1, 128), 1)
    counts = jnp.zeros((1, 128), F32)
    for k in range(shards // don_size):
        counts = jnp.where(lane == don * (shards // don_size) + k, dcnt[k].astype(F32), counts)
    cnt_s[...] = jnp.broadcast_to(counts, cnt_s.shape)
    side = []
    for k, peer in enumerate(others):
        to = lax.rem(peer[0], 2)
        for j, (source, dest) in enumerate(((comb_s.at[to], comb_l.at[don]), (cnt_s, cnt_l.at[don]))):
            copy = pltpu.make_async_remote_copy(
                src_ref=source, dst_ref=dest, send_sem=side_send.at[k, j], recv_sem=side_recv.at[k, j],
                device_id=peer, device_id_type=MESH,
            )
            copy.start()
            side.append(copy)
    comb_l[don] = comb_s[core]
    cnt_l[don] = cnt_s[...]

    rank_a, label_a = acceptor_tables(acnt, shards, slots, sites)
    rank_s[...] = rank_a
    label_s[...] = label_a
    shard_row = lax.broadcasted_iota(I32, (first_s.shape[1], sites), 0)
    slot_lane = lax.broadcasted_iota(I32, (first_s.shape[1], sites), 1)
    before = slot_lane >= (shard_row + 1) * slots
    within_shard = (slot_lane >= shard_row * slots) & jnp.logical_not(before)
    first_s[0] = jnp.where(before, 1.0, 0.0).astype(BF16)
    first_s[1] = jnp.where(within_shard, 1.0, 0.0).astype(BF16)

    rows_live = round_up(live, 16)
    chunk = row_chunk(rows_d)
    if rows_a > rows_live:
        a_s[rows_live:, :] = jnp.zeros((rows_a - rows_live, width), BF16)
        d_s[rows_live:, :] = jnp.zeros((rows_d - rows_live, width), BF16)
        tab_s[:, rows_live:] = jnp.zeros((tab_s.shape[0], rows_d - rows_live), F32)
        for t in range(half):
            p_s[t, rows_live:, :] = jnp.zeros((rows_d - rows_live, width), BF16)
        for t in range(ds_s.shape[0]):
            ds_s[t, rows_live:, :] = jnp.zeros((rows_a - rows_live, rows_d), BF16)


    def stage_four(kind):
        for kx in range(chips):
            for ka in range(acc_size):
                arrived(kind, slot_of((away(x, kx, chips) * 2 + 1 - core, away(acc, ka, acc_size))))

    relays_one(0)
    relays_one(1)
    relays_two(0)
    relays_three(0)
    relays_two(1)
    relays_four(0)
    relays_three(1)

    for copy in side:
        copy.wait()
    counts = cnt_l[0]
    for k in range(1, don_size):
        counts = counts + cnt_l[k]
    counts = counts.astype(BF16)
    first = jnp.dot(counts, first_s[0], preferred_element_type=F32)
    number = jnp.dot(counts, first_s[1], preferred_element_type=F32)
    shard_of = jnp.sum(first_s[0].astype(F32), axis=0, keepdims=True)
    within = lax.broadcasted_iota(I32, (8, sites), 1).astype(F32) - shard_of * slots
    rank_d = jnp.where(within < number, first + within, -1.0).astype(I32)[:1]
    comb = jnp.concatenate([comb_l[k] for k in range(don_size)], axis=1)
    table = jnp.concatenate(
        [(comb & 1).astype(F32), ((comb >> 1) & 255).astype(F32), (comb >> 9).astype(F32)], axis=0
    ).astype(BF16)
    stage_four(0)
    for n in range(0, rows_live, chunk):
        size = min(chunk, rows_live - n)
        span = slice(n, n + size)
        row = lax.broadcasted_iota(I32, (size, sites), 0) + n
        pick = jnp.where(row == rank_d, 1.0, 0.0).astype(BF16)
        d = jnp.dot(pick, xd[...].reshape(sites, width), preferred_element_type=F32)
        d_s[span, :] = d.astype(BF16)
        tab_s[:, span] = contract_last(table, pick)

    weights_in[0].wait()

    def project(t):
        for n in range(0, rows_live, chunk):
            span = slice(n, min(n + chunk, rows_live))
            p_s[t, span, :] = jnp.dot(d_s[span, :], w_s[tissue(t)], preferred_element_type=F32).astype(BF16)

    for t in range(half):
        if t == half // 2:
            relays_four(1)
        project(t)
    for n in range(0, rows_d, chunk):
        span = slice(n, n + chunk)
        dt_s[:, span] = jnp.transpose(d_s[span, :].astype(F32)).astype(BF16)

    stage_four(1)
    for n in range(0, rows_live, chunk):
        size = min(chunk, rows_live - n)
        row = lax.broadcasted_iota(I32, (size, sites), 0) + n
        pick = jnp.where(row == rank_s[:1, :], 1.0, 0.0).astype(BF16)
        a_s[n : n + size, :] = jnp.dot(
            pick, xa[...].reshape(sites, width), preferred_element_type=F32
        ).astype(BF16)

    label_col = jnp.transpose(jnp.broadcast_to(label_s[:1, :rows_a].astype(F32), (128, rows_a)))[:rows_live]
    lost = []
    kept = []

    def hits(t, span):
        goal = tab_s[pl.ds(half + tissue(t), 1), span] + 256.0 * tab_s[pl.ds(2 * half + tissue(t), 1), span]
        return jnp.concatenate([label_col] * (chunk // 128), axis=1) == goal

    deep = e_s.shape[0]

    def score(t):
        for n in range(0, rows_d, chunk):
            span = slice(n, n + chunk)
            raw = contract_last(a_s[:rows_live, :], p_s[t, span, :])
            if rows_live > live:
                row = lax.broadcasted_iota(I32, raw.shape, 0)
                raw = jnp.where(row < live, raw, -1e30)
            weight = tab_s[pl.ds(tissue(t), 1), span]
            highest = jnp.max(raw, axis=0, keepdims=True)
            expo = jnp.exp2((raw - highest) * (scale * LOG2E))
            e_s[t % deep, :, span] = expo
            summed = jnp.sum(expo, axis=0, keepdims=True)
            picked = jnp.sum(jnp.where(hits(t, span), raw, 0.0), axis=0, keepdims=True)
            lost.append(weight * (jnp.log(summed) + scale * (highest - picked)))
            kept.append((t, span, weight, weight / summed))
    at_loss = (lax.rem(x, parts) * 2 + core) * acc_size + acc
    loss_copies = []

    def send_loss():
        num = sum(jnp.sum(part) for part in lost)
        cnt = sum(jnp.sum(weight) for _, _, weight, _ in kept)
        first_row = lax.broadcasted_iota(I32, loss_s.shape, 0) == 0
        loss_s[...] = jnp.where(first_row, num, cnt)
        for k, peer in enumerate(lossers):
            copy = pltpu.make_async_remote_copy(
                src_ref=loss_s, dst_ref=loss_l.at[at_loss], send_sem=loss_send.at[k], recv_sem=loss_recv.at[k],
                device_id=peer, device_id_type=MESH,
            )
            copy.start()
            loss_copies.append(copy)
        loss_l[at_loss] = loss_s[...]

    tot_copies = []

    def back(t):
        for t_at, span, weight, factor in kept:
            if t_at == t:
                prob = e_s[t % deep, :, span] * factor
                ds_s[t % deep, :rows_live, span] = jnp.where(hits(t, span), prob - weight, prob).astype(BF16)
        at = core * half + tissue(t)
        for mine in (False, True):
            which = core if mine else 1 - core
            rows = pl.multiple_of((x * 2 + which) * depth, depth)
            total = contract_last(dt_s[pl.ds(rows, depth), :], ds_s[t % deep]) * scale
            if mine:
                tot_out[at] = total.astype(BF16)
            else:
                tot_s[t] = total.astype(BF16)
                copy = pltpu.make_async_remote_copy(
                    src_ref=tot_s.at[t], dst_ref=tot_out.at[at], send_sem=tot_send.at[t], recv_sem=tot_recv.at[t],
                    device_id=sibling, device_id_type=MESH,
                )
                copy.start()
                tot_copies.append(copy)

    for first in range(0, half, deep):
        for t in range(first, first + deep):
            score(t)
            if t == share - 1:
                send_loss()
        for t in range(first, first + deep):
            back(t)

    def gradient(at):
        grad_out[at] = jnp.dot(tot_out[at], a_s[...], preferred_element_type=F32)

    for t in range(half):
        gradient(core * half + tissue(t))
    for t in range(half):
        tot_copies[t].wait()
        gradient((1 - core) * half + tissue(t))
    for copy in loss_copies:
        copy.wait()
    total = loss_l[0]
    for k in range(1, 2 * parts * acc_size):
        total = total + loss_l[k]
    loss_out[...] = jnp.broadcast_to(total[:1] / jnp.maximum(total[1:2], 1.0), loss_out.shape)
    for copy in sent:
        copy.wait_send()


def main(don_size, acc_size, dpos, apos, dcnt, acnt, demb, aemb, target, mask, weights):
    slots, width = dpos.shape[0], demb.shape[1]
    tis = weights.shape[0]
    half = tis // 2
    shards = don_size * acc_size
    sites = shards * slots
    live = shards * (slots + 1) // 2
    padded = round_up(live, 128)
    depth = width // don_size
    inner = 1
    while (2 * inner) ** 2 <= acc_size:
        inner *= 2
    outer, chips = acc_size // inner, don_size // 2
    sends = shards // 2 + (outer - 1) + outer * inner * chips - outer
    tile_rows = max(8, tis)
    hbm = pl.BlockSpec(memory_space=pltpu.HBM)
    vmem = pl.BlockSpec(memory_space=pltpu.VMEM)
    dma = pltpu.SemaphoreType.DMA
    parts = 1
    lossers = 2 * parts * acc_size - 1
    deep = half if half * padded * padded <= 1 << 21 else 1
    arrays = 2 * width * (2 * demb.shape[0] + half * width + 3 * sites + (3 + half) * padded + tis * depth)
    limit = arrays + arrays // 4 + deep * padded * padded * 6 + (8 << 20)
    return pl.pallas_call(
        functools.partial(main_kernel, don_size, acc_size, inner, live),
        in_specs=[hbm] * 9,
        out_specs=[vmem, vmem],
        out_shape=[
            jax.ShapeDtypeStruct((tis, depth, width), F32),
            jax.ShapeDtypeStruct((8, 128), F32),
        ],
        scratch_shapes=[
            pltpu.SMEM(dpos.shape, I32),
            pltpu.SMEM(apos.shape, I32),
            pltpu.SMEM(dcnt.shape, I32),
            pltpu.SMEM(acnt.shape, I32),
            pltpu.VMEM(demb.shape, BF16),
            pltpu.VMEM(aemb.shape, BF16),
            pltpu.VMEM((half, width, width), BF16),
            pltpu.VMEM((2, tile_rows, sites // don_size), I32),
            pltpu.VMEM((shards, slots, width), BF16),
            pltpu.VMEM((shards, slots, width), BF16),
            pltpu.VMEM((2, half, sites // don_size), I32),
            pltpu.VMEM((don_size, half, sites // don_size), I32),
            pltpu.VMEM((8, 128), F32),
            pltpu.VMEM((don_size, 8, 128), F32),
            pltpu.VMEM((padded, width), BF16),
            pltpu.VMEM((width, padded), BF16),
            pltpu.VMEM((padded, width), BF16),
            pltpu.VMEM((half, padded, width), BF16),
            pltpu.VMEM((deep, round_up(live, 16), padded), F32),
            pltpu.VMEM((deep, padded, padded), BF16),
            pltpu.VMEM((tis, depth, padded), BF16),
            pltpu.VMEM((half, depth, padded), BF16),
            pltpu.VMEM((8, sites), I32),
            pltpu.VMEM((8, sites), I32),
            pltpu.VMEM((3 * half, padded), F32),
            pltpu.VMEM((2, 128, sites), BF16),
            pltpu.VMEM((8, 128), F32),
            pltpu.VMEM((2 * parts * acc_size, 8, 128), F32),
            dma((9,)),
            dma((half,)),
            dma((2, PIECES)),
            dma((2, sends)),
            dma((2, shards)),
            dma((1,)),
            dma((1,)),
            dma((don_size - 1, 2)),
            dma((don_size - 1, 2)),
            dma((half,)),
            dma((half,)),
            dma((lossers,)),
            dma((lossers,)),
        ],
        compiler_params=pltpu.CompilerParams(
            collective_id=0, has_side_effects=True, vmem_limit_bytes=min(limit, 60 << 20)
        ),
    )(*[
        pltpu.with_memory_space_constraint(array, pltpu.HBM)
        for array in (dpos, apos, dcnt, acnt, demb, aemb, target, mask, weights)
    ])


def grad_kernel(buf, loss_ref, grad_ref, out_ref, sem):
    copies = []
    for t in range(buf.shape[0]):
        copy = pltpu.make_async_copy(buf.at[t], grad_ref.at[:, t, :], sem.at[t])
        copy.start()
        copies.append(copy)
    out_ref[0, 0] = jnp.max(loss_ref[...])
    for copy in copies:
        copy.wait()


def grad(by_tissue, loss):
    tis, depth, width = by_tissue.shape
    vmem = pl.BlockSpec(memory_space=pltpu.VMEM)
    return pl.pallas_call(
        grad_kernel,
        in_specs=[vmem, vmem],
        out_specs=[pl.BlockSpec(memory_space=pl.ANY), pl.BlockSpec(memory_space=pltpu.SMEM)],
        out_shape=[jax.ShapeDtypeStruct((depth, tis, width), F32), jax.ShapeDtypeStruct((1, 1), F32)],
        scratch_shapes=[pltpu.SemaphoreType.DMA((tis,))],
        compiler_params=pltpu.CompilerParams(vmem_limit_bytes=8 << 20),
    )(by_tissue, loss)


def local(
    don_size, acc_size, donor_emb, acceptor_emb, donor_pos, acceptor_pos, donor_count, acceptor_count,
    target, junction_mask, weights,
):
    by_tissue, loss = main(
        don_size, acc_size, donor_pos, acceptor_pos, donor_count, acceptor_count,
        donor_emb, acceptor_emb, target, junction_mask, weights,
    )
    grad_weight, loss = grad(by_tissue, loss)
    return loss.reshape(()), grad_weight


def solution(mesh):
    return jax.shard_map(
        functools.partial(local, mesh.shape["don"], mesh.shape["acc"]),
        mesh=mesh,
        in_specs=(
            P(("don", "acc"), None),
            P(("don", "acc"), None),
            P(("don", "acc")),
            P(("don", "acc")),
            P("don"),
            P(),
            P(None, "don"),
            P(None, "don"),
            P("acc", None, None),
        ),
        out_specs=(P(), P("don", "acc", None)),
        check_vma=False,
    )
```

```python
import functools
import itertools
import math

import jax
import jax.numpy as jnp
from jax import lax
from jax.experimental import pallas as pl
from jax.experimental.pallas import tpu as pltpu
from jax.sharding import PartitionSpec as P

BF16 = jnp.bfloat16
F32 = jnp.float32
I32 = jnp.int32
MESH = pl.DeviceIdType.MESH
PIECES = 4
LOG2E = 1.4426950408889634


def round_up(n, m):
    return (n + m - 1) // m * m


def row_chunk(n, limit=512):
    best = 128
    for r in range(128, limit + 1, 128):
        if n % r == 0:
            best = r
    return best


def contract_last(a, b):
    return lax.dot_general(a, b, (((1,), (1,)), ((), ())), preferred_element_type=F32)


def acceptor_tables(counts, shards, slots, width):
    col = lax.broadcasted_iota(I32, (8, width), 1)

    def step(k, carry):
        first, rank, label = carry
        number = counts[k]
        within = col - k * slots
        live = (within >= 0) & (within < number)
        rank = jnp.where(live, first + within, rank)
        last = first + number
        return last, rank, label + jnp.where(col >= last, slots - number, 0)

    return lax.fori_loop(0, shards, step, (jnp.int32(0), jnp.full((8, width), -1, I32), col))[1:]


def main_kernel(
    don_size, acc_size, inner, live,
    dpos_h, apos_h, dcnt_h, acnt_h, demb, aemb, target, mask, weights,
    grad_out, loss_out,
    dpos, apos, dcnt, acnt, demb_v, aemb_v, w_s, tm_s, xd, xa, comb_s, comb_l, cnt_s, cnt_l,
    d_s, dt_s, a_s, p_s, e_s, ds_s, tot_out, tot_s, rank_s, label_s, tab_s, first_s, loss_s, loss_l,
    in_sem, w_sem, row_sem, send_sem, recv_sem, sib_send, sib_recv, side_send, side_recv,
    tot_send, tot_recv, loss_send, loss_recv,
):
    shards, slots, width = xd.shape
    outer, chips = acc_size // inner, don_size // 2
    sites = shards * slots
    don_sites = sites // don_size
    half, rows_d = w_s.shape[0], d_s.shape[0]
    rows_a = a_s.shape[0]
    depth = width // don_size
    tis = 2 * half
    scale = width ** (-0.5)
    alternate = chips == inner
    don, acc = lax.axis_index("don"), lax.axis_index("acc")
    core, x = lax.rem(don, 2), don // 2
    o, i = acc // inner, lax.rem(acc, inner)
    if alternate:
        b = core * x + (1 - core) * i
        c = core * i + (1 - core) * x
        b_size, c_size = inner, inner
    else:
        b, c, b_size, c_size = i, x, inner, chips

    def place(oo, bb, cc):
        if alternate:
            xx = core * bb + (1 - core) * cc
            ii = core * cc + (1 - core) * bb
        else:
            xx, ii = cc, bb
        return (xx * 2 + core, oo * inner + ii)

    def away(at, k, size):
        return lax.rem(at + k, size)

    def near(at, k, size):
        up = k - 1 + jnp.where(k - 1 >= at, 1, 0)
        down = k - 1 + jnp.where(k - 1 >= size - 1 - at, 1, 0)
        return jnp.where(2 * at < size, up, size - 1 - down)

    def slot_of(at):
        return at[0] * acc_size + at[1]

    sibling = (x * 2 + 1 - core, acc)
    tile_rows = tm_s.shape[1]
    row_at = pl.multiple_of(acc * tis // tile_rows * tile_rows, tile_rows)
    copies = [
        None,
        pltpu.make_async_copy(target.at[pl.ds(row_at, tile_rows), :], tm_s.at[0], in_sem.at[1]),
        pltpu.make_async_copy(mask.at[pl.ds(row_at, tile_rows), :], tm_s.at[1], in_sem.at[2]),
        None,
        None,
    ]
    weights_in = [pltpu.make_async_copy(weights.at[pl.ds(core * half, half)], w_s, w_sem.at[0])]
    small = [
        pltpu.make_async_copy(source, dest, in_sem.at[5 + k])
        for k, (source, dest) in enumerate(((dpos_h, dpos), (apos_h, apos), (dcnt_h, dcnt), (acnt_h, acnt)))
    ]
    piece = demb_v.shape[0] // PIECES
    rows_in = [
        [
            pltpu.make_async_copy(
                emb.at[pl.ds(n * piece, piece), :], emb_v.at[pl.ds(n * piece, piece), :], row_sem.at[which, n]
            )
            for n in range(PIECES)
        ]
        for which, (emb, emb_v) in enumerate(((demb, demb_v), (aemb, aemb_v)))
    ]
    for copy in small[:2] + rows_in[0] + small[2:] + copies[1:3]:
        copy.start()

    others = [(away(don, k, don_size), acc) for k in range(1, don_size)]
    lossers = [
        (x * 2 + away(core, kc, 2), away(acc, ka, acc_size))
        for kc in range(2) for ka in range(acc_size) if kc or ka
    ]
    direct = others + [(don, away(o, k, outer) * inner + i) for k in range(1, outer)]
    direct += [(don, o * inner + away(i, k, inner)) for k in range(1, inner)]
    barrier = pltpu.get_barrier_semaphore()
    for peer in direct:
        pl.semaphore_signal(barrier, inc=1, device_id=peer, device_id_type=MESH)

    def own_rows(pos, which, landing):
        emb_v = (demb_v, aemb_v)[which]
        small[which].wait()
        row = lax.broadcasted_iota(I32, (slots, 128), 0)
        want = jnp.zeros((slots, 128), I32)
        for k in range(slots):
            want = jnp.where(row == k, pos[k], want)
        col = lax.broadcasted_iota(I32, (slots, piece), 1)
        want = jnp.concatenate([want] * (piece // 128), axis=1)
        rows = jnp.zeros((slots, width), F32)
        for n in range(PIECES):
            pick = jnp.where(col + n * piece == want, 1.0, 0.0).astype(BF16)
            rows_in[which][n].wait()
            rows = rows + jnp.dot(pick, emb_v[n * piece : (n + 1) * piece, :], preferred_element_type=F32)
        landing[held] = rows.astype(BF16)

    held = don * acc_size + acc
    own_rows(dpos, 0, xd)
    pl.semaphore_wait(barrier, len(direct))

    sent = []
    land = (xd, xa)

    def send(kind, source, slot, peer, count):
        n = count[kind]
        count[kind] += 1
        copy = pltpu.make_async_remote_copy(
            src_ref=source, dst_ref=land[kind].at[slot],
            send_sem=send_sem.at[kind, n], recv_sem=recv_sem.at[kind, slot],
            device_id=peer, device_id_type=MESH,
        )
        copy.start()
        sent.append(copy)

    def arrived(kind, slot):
        pltpu.make_async_copy(land[kind].at[slot], land[kind].at[slot], recv_sem.at[kind, slot]).wait()

    counter = [0, 0]

    def at_offset(ko, kb, kc):
        return place(near(o, ko, outer) if ko else o, away(b, kb, b_size), away(c, kc, c_size))

    def targets(ko, kb, kc):
        line = [(k, 0, 0) for k in range(outer - 1, 0, -1)]
        along_b = [(0, k, 0) for k in range(1, b_size)]
        along_c = [(0, 0, k) for k in range(1, c_size)]
        return [] if kc else along_c if kb else along_b + along_c if ko else line + along_b + along_c

    def forward(kind, offset):
        slot = slot_of(at_offset(*offset))
        for hop in targets(*offset):
            send(kind, land[kind].at[slot], slot, at_offset(*hop), counter)
        send(kind, land[kind].at[slot], slot, sibling, counter)

    def relay(kind, offset):
        arrived(kind, slot_of(at_offset(*offset)))
        forward(kind, offset)

    every = list(itertools.product(range(outer), range(b_size), range(c_size)))
    relayed = set()

    def relays(kind, chosen):
        for offset in every:
            if any(offset) and chosen(*offset) and (kind, offset) not in relayed:
                relayed.add((kind, offset))
                relay(kind, offset)

    def relays_one(kind):
        relays(kind, lambda ko, kb, kc: not ko and not kc)
        relays(kind, lambda ko, kb, kc: not kb and not kc)

    def relays_two(kind):
        relays(kind, lambda ko, kb, kc: ko and not kc)

    def relays_three(kind):
        relays(kind, lambda ko, kb, kc: not kb)

    def relays_four(kind):
        relays(kind, lambda ko, kb, kc: True)

    forward(0, (0, 0, 0))
    for copy in rows_in[1]:
        copy.start()
    own_rows(apos, 1, xa)
    forward(1, (0, 0, 0))
    for copy in weights_in:
        copy.start()
    copies[1].wait()
    copies[2].wait()
    both = tm_s[0] * 2 + tm_s[1]
    for core_at in range(2):
        mine = both[core_at * half : (core_at + 1) * half]
        for k in range(1, tile_rows // tis):
            at = k * tis + core_at * half
            mine = jnp.where(lax.rem(acc, tile_rows // tis) == k, both[at : at + half], mine)
        comb_s[core_at] = jnp.concatenate([mine] * (comb_s.shape[1] // half), axis=0)

    for copy in small[2:]:
        copy.wait()
    lane = lax.broadcasted_iota(I32, (1, 128), 1)
    counts = jnp.zeros((1, 128), F32)
    for k in range(shards // don_size):
        counts = jnp.where(lane == don * (shards // don_size) + k, dcnt[k].astype(F32), counts)
    cnt_s[...] = jnp.broadcast_to(counts, cnt_s.shape)
    side = []
    for k, peer in enumerate(others):
        to = lax.rem(peer[0], 2)
        for j, (source, dest) in enumerate(((comb_s.at[to], comb_l.at[don]), (cnt_s, cnt_l.at[don]))):
            copy = pltpu.make_async_remote_copy(
                src_ref=source, dst_ref=dest, send_sem=side_send.at[k, j], recv_sem=side_recv.at[k, j],
                device_id=peer, device_id_type=MESH,
            )
            copy.start()
            side.append(copy)
    comb_l[don] = comb_s[core]
    cnt_l[don] = cnt_s[...]

    rank_a, label_a = acceptor_tables(acnt, shards, slots, sites)
    rank_s[...] = rank_a
    label_s[...] = label_a
    shard_row = lax.broadcasted_iota(I32, (first_s.shape[1], sites), 0)
    slot_lane = lax.broadcasted_iota(I32, (first_s.shape[1], sites), 1)
    before = slot_lane >= (shard_row + 1) * slots
    within_shard = (slot_lane >= shard_row * slots) & jnp.logical_not(before)
    first_s[0] = jnp.where(before, 1.0, 0.0).astype(BF16)
    first_s[1] = jnp.where(within_shard, 1.0, 0.0).astype(BF16)

    rows_live = round_up(live, 16)
    chunk = row_chunk(rows_d)
    if rows_a > rows_live:
        a_s[rows_live:, :] = jnp.zeros((rows_a - rows_live, width), BF16)
        d_s[rows_live:, :] = jnp.zeros((rows_d - rows_live, width), BF16)
        tab_s[:, rows_live:] = jnp.zeros((tab_s.shape[0], rows_d - rows_live), F32)
        for t in range(half):
            p_s[t, rows_live:, :] = jnp.zeros((rows_d - rows_live, width), BF16)
        for t in range(ds_s.shape[0]):
            ds_s[t, rows_live:, :] = jnp.zeros((rows_a - rows_live, rows_d), BF16)


    def stage_four(kind):
        for kx in range(chips):
            for ka in range(acc_size):
                arrived(kind, slot_of((away(x, kx, chips) * 2 + 1 - core, away(acc, ka, acc_size))))

    relays_one(0)
    relays_one(1)
    relays_two(0)
    relays_three(0)
    relays_two(1)
    relays_four(0)
    relays_three(1)

    for copy in side:
        copy.wait()
    counts = cnt_l[0]
    for k in range(1, don_size):
        counts = counts + cnt_l[k]
    counts = counts.astype(BF16)
    first = jnp.dot(counts, first_s[0], preferred_element_type=F32)
    number = jnp.dot(counts, first_s[1], preferred_element_type=F32)
    shard_of = jnp.sum(first_s[0].astype(F32), axis=0, keepdims=True)
    within = lax.broadcasted_iota(I32, (8, sites), 1).astype(F32) - shard_of * slots
    rank_d = jnp.where(within < number, first + within, -1.0).astype(I32)[:1]
    comb = jnp.concatenate([comb_l[k] for k in range(don_size)], axis=1)
    table = jnp.concatenate(
        [(comb & 1).astype(F32), ((comb >> 1) & 255).astype(F32), (comb >> 9).astype(F32)], axis=0
    ).astype(BF16)
    stage_four(0)
    for n in range(0, rows_live, chunk):
        size = min(chunk, rows_live - n)
        span = slice(n, n + size)
        row = lax.broadcasted_iota(I32, (size, sites), 0) + n
        pick = jnp.where(row == rank_d, 1.0, 0.0).astype(BF16)
        d = jnp.dot(pick, xd[...].reshape(sites, width), preferred_element_type=F32)
        d_s[span, :] = d.astype(BF16)
        tab_s[:, span] = contract_last(table, pick)

    weights_in[0].wait()

    def project(t):
        for n in range(0, rows_live, chunk):
            span = slice(n, min(n + chunk, rows_live))
            p_s[t, span, :] = jnp.dot(d_s[span, :], w_s[t], preferred_element_type=F32).astype(BF16)

    for t in range(half):
        if t == half // 2:
            relays_four(1)
        project(t)
    for n in range(0, rows_d, chunk):
        span = slice(n, n + chunk)
        dt_s[:, span] = jnp.transpose(d_s[span, :].astype(F32)).astype(BF16)

    stage_four(1)
    for n in range(0, rows_live, chunk):
        size = min(chunk, rows_live - n)
        row = lax.broadcasted_iota(I32, (size, sites), 0) + n
        pick = jnp.where(row == rank_s[:1, :], 1.0, 0.0).astype(BF16)
        a_s[n : n + size, :] = jnp.dot(
            pick, xa[...].reshape(sites, width), preferred_element_type=F32
        ).astype(BF16)

    label_col = jnp.transpose(jnp.broadcast_to(label_s[:1, :rows_a].astype(F32), (128, rows_a)))[:rows_live]
    lost = []
    kept = []

    group = comb_s.shape[1]

    def hits(t, span):
        goal = tab_s[pl.ds(group + t, 1), span] + 256.0 * tab_s[pl.ds(2 * group + t, 1), span]
        return jnp.concatenate([label_col] * (chunk // 128), axis=1) == goal

    deep = e_s.shape[0]

    def score(t):
        for n in range(0, rows_d, chunk):
            span = slice(n, n + chunk)
            raw = contract_last(a_s[:rows_live, :], p_s[t, span, :])
            if rows_live > live:
                row = lax.broadcasted_iota(I32, raw.shape, 0)
                raw = jnp.where(row < live, raw, -1e30)
            weight = tab_s[pl.ds(t, 1), span]
            highest = jnp.max(raw, axis=0, keepdims=True)
            expo = jnp.exp2((raw - highest) * (scale * LOG2E))
            e_s[t % deep, :, span] = expo
            summed = jnp.sum(expo, axis=0, keepdims=True)
            picked = jnp.sum(jnp.where(hits(t, span), raw, 0.0), axis=0, keepdims=True)
            lost.append(weight * (jnp.log(summed) + scale * (highest - picked)))
            kept.append((t, span, weight, weight / summed))
    at_loss = core * acc_size + acc
    loss_copies = []

    def send_loss():
        def lanes(parts):
            whole = sum(parts[1:], parts[0])
            pieces = [whole[:, n : n + 128] for n in range(0, whole.shape[1], 128)]
            return sum(pieces[1:], pieces[0])

        num, cnt = lanes(lost), lanes([weight for _, _, weight, _ in kept])
        first_row = lax.broadcasted_iota(I32, loss_s.shape, 0) == 0
        loss_s[...] = jnp.where(first_row, num, cnt)
        for k, peer in enumerate(lossers):
            copy = pltpu.make_async_remote_copy(
                src_ref=loss_s, dst_ref=loss_l.at[at_loss], send_sem=loss_send.at[k], recv_sem=loss_recv.at[k],
                device_id=peer, device_id_type=MESH,
            )
            copy.start()
            loss_copies.append(copy)
        loss_l[at_loss] = loss_s[...]

    tot_copies = []

    def back(t):
        for t_at, span, weight, factor in kept:
            if t_at == t:
                prob = e_s[t % deep, :, span] * factor
                ds_s[t % deep, :rows_live, span] = jnp.where(hits(t, span), prob - weight, prob).astype(BF16)
        at = core * half + t
        for mine in (False, True):
            which = core if mine else 1 - core
            rows = pl.multiple_of((x * 2 + which) * depth, depth)
            total = contract_last(dt_s[pl.ds(rows, depth), :], ds_s[t % deep]) * scale
            if mine:
                tot_out[at] = total.astype(BF16)
            else:
                tot_s[t] = total.astype(BF16)
                copy = pltpu.make_async_remote_copy(
                    src_ref=tot_s.at[t], dst_ref=tot_out.at[at], send_sem=tot_send.at[t], recv_sem=tot_recv.at[t],
                    device_id=sibling, device_id_type=MESH,
                )
                copy.start()
                tot_copies.append(copy)

    for first in range(0, half, deep):
        for t in range(first, first + deep):
            score(t)
            if t == half - 1:
                send_loss()
        for t in range(first, first + deep):
            back(t)

    def gradient(at):
        grad_out[at] = jnp.dot(tot_out[at], a_s[...], preferred_element_type=F32)

    for t in range(half):
        gradient(core * half + t)
    for t in range(half):
        tot_copies[t].wait()
        gradient((1 - core) * half + t)
    for copy in sent:
        copy.wait_send()
    for copy in loss_copies:
        copy.wait()
    total = loss_l[0]
    for k in range(1, 2 * acc_size):
        total = total + loss_l[k]
    total = jnp.sum(total, axis=1, keepdims=True)
    loss_out[...] = jnp.broadcast_to(total[:1] / jnp.maximum(total[1:2], 1.0), loss_out.shape)


def main(don_size, acc_size, dpos, apos, dcnt, acnt, demb, aemb, target, mask, weights):
    slots, width = dpos.shape[0], demb.shape[1]
    tis = weights.shape[0]
    half = tis // 2
    shards = don_size * acc_size
    sites = shards * slots
    live = shards * (slots + 1) // 2
    padded = round_up(live, 128)
    depth = width // don_size
    inner = 1
    while (2 * inner) ** 2 <= acc_size:
        inner *= 2
    outer, chips = acc_size // inner, don_size // 2
    sends = shards // 2 + (outer - 1) + outer * inner * chips - outer
    tile_rows = max(8, tis)
    hbm = pl.BlockSpec(memory_space=pltpu.HBM)
    vmem = pl.BlockSpec(memory_space=pltpu.VMEM)
    dma = pltpu.SemaphoreType.DMA
    lossers = 2 * acc_size - 1
    deep = half if half * padded * padded <= 1 << 21 else 1
    arrays = 2 * width * (2 * demb.shape[0] + half * width + 3 * sites + (3 + half) * padded + tis * depth)
    limit = arrays + arrays // 4 + deep * padded * padded * 6 + (8 << 20)
    return pl.pallas_call(
        functools.partial(main_kernel, don_size, acc_size, inner, live),
        in_specs=[hbm] * 9,
        out_specs=[vmem, vmem],
        out_shape=[
            jax.ShapeDtypeStruct((tis, depth, width), F32),
            jax.ShapeDtypeStruct((8, 128), F32),
        ],
        scratch_shapes=[
            pltpu.SMEM(dpos.shape, I32),
            pltpu.SMEM(apos.shape, I32),
            pltpu.SMEM(dcnt.shape, I32),
            pltpu.SMEM(acnt.shape, I32),
            pltpu.VMEM(demb.shape, BF16),
            pltpu.VMEM(aemb.shape, BF16),
            pltpu.VMEM((half, width, width), BF16),
            pltpu.VMEM((2, tile_rows, sites // don_size), I32),
            pltpu.VMEM((shards, slots, width), BF16),
            pltpu.VMEM((shards, slots, width), BF16),
            pltpu.VMEM((2, max(8, half), sites // don_size), I32),
            pltpu.VMEM((don_size, max(8, half), sites // don_size), I32),
            pltpu.VMEM((8, 128), F32),
            pltpu.VMEM((don_size, 8, 128), F32),
            pltpu.VMEM((padded, width), BF16),
            pltpu.VMEM((width, padded), BF16),
            pltpu.VMEM((padded, width), BF16),
            pltpu.VMEM((half, padded, width), BF16),
            pltpu.VMEM((deep, round_up(live, 16), padded), F32),
            pltpu.VMEM((deep, padded, padded), BF16),
            pltpu.VMEM((tis, depth, padded), BF16),
            pltpu.VMEM((half, depth, padded), BF16),
            pltpu.VMEM((8, sites), I32),
            pltpu.VMEM((8, sites), I32),
            pltpu.VMEM((3 * max(8, half), padded), F32),
            pltpu.VMEM((2, 128, sites), BF16),
            pltpu.VMEM((8, 128), F32),
            pltpu.VMEM((2 * acc_size, 8, 128), F32),
            dma((9,)),
            dma((half,)),
            dma((2, PIECES)),
            dma((2, sends)),
            dma((2, shards)),
            dma((1,)),
            dma((1,)),
            dma((don_size - 1, 2)),
            dma((don_size - 1, 2)),
            dma((half,)),
            dma((half,)),
            dma((lossers,)),
            dma((lossers,)),
        ],
        compiler_params=pltpu.CompilerParams(
            collective_id=0, has_side_effects=True, vmem_limit_bytes=min(limit, 60 << 20)
        ),
    )(*[
        pltpu.with_memory_space_constraint(array, pltpu.HBM)
        for array in (dpos, apos, dcnt, acnt, demb, aemb, target, mask, weights)
    ])


def grad_kernel(buf, loss_ref, grad_ref, out_ref, sem):
    copies = []
    for t in range(buf.shape[0]):
        copy = pltpu.make_async_copy(buf.at[t], grad_ref.at[:, t, :], sem.at[t])
        copy.start()
        copies.append(copy)
    out_ref[0, 0] = jnp.max(loss_ref[...])
    for copy in copies:
        copy.wait()


def grad(by_tissue, loss):
    tis, depth, width = by_tissue.shape
    vmem = pl.BlockSpec(memory_space=pltpu.VMEM)
    return pl.pallas_call(
        grad_kernel,
        in_specs=[vmem, vmem],
        out_specs=[pl.BlockSpec(memory_space=pl.ANY), pl.BlockSpec(memory_space=pltpu.SMEM)],
        out_shape=[jax.ShapeDtypeStruct((depth, tis, width), F32), jax.ShapeDtypeStruct((1, 1), F32)],
        scratch_shapes=[pltpu.SemaphoreType.DMA((tis,))],
        compiler_params=pltpu.CompilerParams(vmem_limit_bytes=8 << 20),
    )(by_tissue, loss)


def local(
    don_size, acc_size, donor_emb, acceptor_emb, donor_pos, acceptor_pos, donor_count, acceptor_count,
    target, junction_mask, weights,
):
    by_tissue, loss = main(
        don_size, acc_size, donor_pos, acceptor_pos, donor_count, acceptor_count,
        donor_emb, acceptor_emb, target, junction_mask, weights,
    )
    grad_weight, loss = grad(by_tissue, loss)
    return loss.reshape(()), grad_weight


def solution(mesh):
    return jax.shard_map(
        functools.partial(local, mesh.shape["don"], mesh.shape["acc"]),
        mesh=mesh,
        in_specs=(
            P(("don", "acc"), None),
            P(("don", "acc"), None),
            P(("don", "acc")),
            P(("don", "acc")),
            P("don"),
            P(),
            P(None, "don"),
            P(None, "don"),
            P("acc", None, None),
        ),
        out_specs=(P(), P("don", "acc", None)),
        check_vma=False,
    )
```

```python
import functools
import itertools
import math

import jax
import jax.numpy as jnp
from jax import lax
from jax.experimental import pallas as pl
from jax.experimental.pallas import tpu as pltpu
from jax.sharding import PartitionSpec as P

BF16 = jnp.bfloat16
F32 = jnp.float32
I32 = jnp.int32
MESH = pl.DeviceIdType.MESH
PIECES = 4
LOG2E = 1.4426950408889634


def round_up(n, m):
    return (n + m - 1) // m * m


def row_chunk(n, limit=512):
    best = 128
    for r in range(128, limit + 1, 128):
        if n % r == 0:
            best = r
    return best


def contract_last(a, b):
    return lax.dot_general(a, b, (((1,), (1,)), ((), ())), preferred_element_type=F32)


def acceptor_tables(counts, shards, slots, width):
    col = lax.broadcasted_iota(I32, (8, width), 1)

    def step(k, carry):
        first, rank, label = carry
        number = counts[k]
        within = col - k * slots
        live = (within >= 0) & (within < number)
        rank = jnp.where(live, first + within, rank)
        last = first + number
        return last, rank, label + jnp.where(col >= last, slots - number, 0)

    return lax.fori_loop(0, shards, step, (jnp.int32(0), jnp.full((8, width), -1, I32), col))[1:]


def main_kernel(
    don_size, acc_size, inner, live,
    dpos_h, apos_h, dcnt_h, acnt_h, demb, aemb, target, mask, weights,
    grad_out, loss_out,
    dpos, apos, dcnt, acnt, demb_v, aemb_v, w_s, tm_s, xd, xa, comb_s, comb_l, cnt_s, cnt_l,
    d_s, dt_s, a_s, p_s, e_s, ds_s, tot_out, tot_s, rank_s, label_s, tab_s, first_s, loss_s, loss_l,
    in_sem, w_sem, row_sem, send_sem, recv_sem, sib_send, sib_recv, side_send, side_recv,
    tot_send, tot_recv, loss_send, loss_recv,
):
    shards, slots, width = xd.shape
    outer, chips = acc_size // inner, don_size // 2
    sites = shards * slots
    don_sites = sites // don_size
    half, rows_d = w_s.shape[0], d_s.shape[0]
    rows_a = a_s.shape[0]
    depth = width // don_size
    tis = 2 * half
    scale = width ** (-0.5)
    alternate = chips == inner
    don, acc = lax.axis_index("don"), lax.axis_index("acc")
    core, x = lax.rem(don, 2), don // 2
    o, i = acc // inner, lax.rem(acc, inner)
    if alternate:
        b = core * x + (1 - core) * i
        c = core * i + (1 - core) * x
        b_size, c_size = inner, inner
    else:
        b, c, b_size, c_size = i, x, inner, chips

    def place(oo, bb, cc):
        if alternate:
            xx = core * bb + (1 - core) * cc
            ii = core * cc + (1 - core) * bb
        else:
            xx, ii = cc, bb
        return (xx * 2 + core, oo * inner + ii)

    def away(at, k, size):
        return lax.rem(at + k, size)

    def near(at, k, size):
        up = k - 1 + jnp.where(k - 1 >= at, 1, 0)
        down = k - 1 + jnp.where(k - 1 >= size - 1 - at, 1, 0)
        return jnp.where(2 * at < size, up, size - 1 - down)

    def slot_of(at):
        return at[0] * acc_size + at[1]

    sibling = (x * 2 + 1 - core, acc)
    tile_rows = tm_s.shape[1]
    row_at = pl.multiple_of(acc * tis // tile_rows * tile_rows, tile_rows)
    copies = [
        None,
        pltpu.make_async_copy(target.at[pl.ds(row_at, tile_rows), :], tm_s.at[0], in_sem.at[1]),
        pltpu.make_async_copy(mask.at[pl.ds(row_at, tile_rows), :], tm_s.at[1], in_sem.at[2]),
        None,
        None,
    ]
    weights_in = [pltpu.make_async_copy(weights.at[pl.ds(core * half, half)], w_s, w_sem.at[0])]
    small = [
        pltpu.make_async_copy(source, dest, in_sem.at[5 + k])
        for k, (source, dest) in enumerate(((dpos_h, dpos), (apos_h, apos), (dcnt_h, dcnt), (acnt_h, acnt)))
    ]
    piece = demb_v.shape[0] // PIECES
    rows_in = [
        [
            pltpu.make_async_copy(
                emb.at[pl.ds(n * piece, piece), :], emb_v.at[pl.ds(n * piece, piece), :], row_sem.at[which, n]
            )
            for n in range(PIECES)
        ]
        for which, (emb, emb_v) in enumerate(((demb, demb_v), (aemb, aemb_v)))
    ]
    for copy in small[:2] + rows_in[0] + small[2:] + copies[1:3]:
        copy.start()

    others = [(away(don, k, don_size), acc) for k in range(1, don_size)]
    lossers = [
        (x * 2 + away(core, kc, 2), (near(o, ko, outer) if ko else o) * inner + away(i, ki, inner))
        for ko in range(outer - 1, -1, -1) for ki in range(inner - 1, -1, -1) for kc in (1, 0) if ko or ki or kc
    ]
    direct = others + [(don, away(o, k, outer) * inner + i) for k in range(1, outer)]
    direct += [(don, o * inner + away(i, k, inner)) for k in range(1, inner)]
    barrier = pltpu.get_barrier_semaphore()
    for peer in direct:
        pl.semaphore_signal(barrier, inc=1, device_id=peer, device_id_type=MESH)

    def own_rows(pos, which, landing):
        emb_v = (demb_v, aemb_v)[which]
        small[which].wait()
        row = lax.broadcasted_iota(I32, (slots, 128), 0)
        want = jnp.zeros((slots, 128), I32)
        for k in range(slots):
            want = jnp.where(row == k, pos[k], want)
        col = lax.broadcasted_iota(I32, (slots, piece), 1)
        want = jnp.concatenate([want] * (piece // 128), axis=1)
        rows = jnp.zeros((slots, width), F32)
        for n in range(PIECES):
            pick = jnp.where(col + n * piece == want, 1.0, 0.0).astype(BF16)
            rows_in[which][n].wait()
            rows = rows + jnp.dot(pick, emb_v[n * piece : (n + 1) * piece, :], preferred_element_type=F32)
        landing[held] = rows.astype(BF16)

    held = don * acc_size + acc
    own_rows(dpos, 0, xd)
    pl.semaphore_wait(barrier, len(direct))

    sent = []
    land = (xd, xa)

    def send(kind, source, slot, peer, count):
        n = count[kind]
        count[kind] += 1
        copy = pltpu.make_async_remote_copy(
            src_ref=source, dst_ref=land[kind].at[slot],
            send_sem=send_sem.at[kind, n], recv_sem=recv_sem.at[kind, slot],
            device_id=peer, device_id_type=MESH,
        )
        copy.start()
        sent.append(copy)

    def arrived(kind, slot):
        pltpu.make_async_copy(land[kind].at[slot], land[kind].at[slot], recv_sem.at[kind, slot]).wait()

    counter = [0, 0]

    def at_offset(ko, kb, kc):
        return place(near(o, ko, outer) if ko else o, away(b, kb, b_size), away(c, kc, c_size))

    def targets(ko, kb, kc):
        line = [(k, 0, 0) for k in range(outer - 1, 0, -1)]
        along_b = [(0, k, 0) for k in range(1, b_size)]
        along_c = [(0, 0, k) for k in range(1, c_size)]
        return [] if kc else along_c if kb else along_b + along_c if ko else line + along_b + along_c

    def forward(kind, offset):
        slot = slot_of(at_offset(*offset))
        for hop in targets(*offset):
            send(kind, land[kind].at[slot], slot, at_offset(*hop), counter)
        send(kind, land[kind].at[slot], slot, sibling, counter)

    def relay(kind, offset):
        arrived(kind, slot_of(at_offset(*offset)))
        forward(kind, offset)

    every = list(itertools.product(range(outer), range(b_size), range(c_size)))
    relayed = set()

    def relays(kind, chosen):
        for offset in every:
            if any(offset) and chosen(*offset) and (kind, offset) not in relayed:
                relayed.add((kind, offset))
                relay(kind, offset)

    def relays_one(kind):
        relays(kind, lambda ko, kb, kc: not ko and not kc)
        relays(kind, lambda ko, kb, kc: not kb and not kc)

    def relays_two(kind):
        relays(kind, lambda ko, kb, kc: ko and not kc)

    def relays_three(kind):
        relays(kind, lambda ko, kb, kc: not kb)

    def relays_four(kind):
        relays(kind, lambda ko, kb, kc: True)

    forward(0, (0, 0, 0))
    for copy in rows_in[1]:
        copy.start()
    own_rows(apos, 1, xa)
    forward(1, (0, 0, 0))
    for copy in weights_in:
        copy.start()
    copies[1].wait()
    copies[2].wait()
    both = tm_s[0] * 2 + tm_s[1]
    for core_at in range(2):
        mine = both[core_at * half : (core_at + 1) * half]
        for k in range(1, tile_rows // tis):
            at = k * tis + core_at * half
            mine = jnp.where(lax.rem(acc, tile_rows // tis) == k, both[at : at + half], mine)
        comb_s[core_at] = jnp.concatenate([mine] * (comb_s.shape[1] // half), axis=0)

    for copy in small[2:]:
        copy.wait()
    lane = lax.broadcasted_iota(I32, (1, 128), 1)
    counts = jnp.zeros((1, 128), F32)
    for k in range(shards // don_size):
        counts = jnp.where(lane == don * (shards // don_size) + k, dcnt[k].astype(F32), counts)
    cnt_s[...] = jnp.broadcast_to(counts, cnt_s.shape)
    side = []
    for k, peer in enumerate(others):
        to = lax.rem(peer[0], 2)
        for j, (source, dest) in enumerate(((comb_s.at[to], comb_l.at[don]), (cnt_s, cnt_l.at[don]))):
            copy = pltpu.make_async_remote_copy(
                src_ref=source, dst_ref=dest, send_sem=side_send.at[k, j], recv_sem=side_recv.at[k, j],
                device_id=peer, device_id_type=MESH,
            )
            copy.start()
            side.append(copy)
    comb_l[don] = comb_s[core]
    cnt_l[don] = cnt_s[...]

    rank_a, label_a = acceptor_tables(acnt, shards, slots, sites)
    rank_s[...] = rank_a
    label_s[...] = label_a
    shard_row = lax.broadcasted_iota(I32, (first_s.shape[1], sites), 0)
    slot_lane = lax.broadcasted_iota(I32, (first_s.shape[1], sites), 1)
    before = slot_lane >= (shard_row + 1) * slots
    within_shard = (slot_lane >= shard_row * slots) & jnp.logical_not(before)
    first_s[0] = jnp.where(before, 1.0, 0.0).astype(BF16)
    first_s[1] = jnp.where(within_shard, 1.0, 0.0).astype(BF16)

    rows_live = round_up(live, 16)
    chunk = row_chunk(rows_d)
    if rows_a > rows_live:
        a_s[rows_live:, :] = jnp.zeros((rows_a - rows_live, width), BF16)
        d_s[rows_live:, :] = jnp.zeros((rows_d - rows_live, width), BF16)
        tab_s[:, rows_live:] = jnp.zeros((tab_s.shape[0], rows_d - rows_live), F32)
        for t in range(half):
            p_s[t, rows_live:, :] = jnp.zeros((rows_d - rows_live, width), BF16)
        for t in range(ds_s.shape[0]):
            ds_s[t, rows_live:, :] = jnp.zeros((rows_a - rows_live, rows_d), BF16)


    def stage_four(kind):
        for kx in range(chips):
            for ka in range(acc_size):
                arrived(kind, slot_of((away(x, kx, chips) * 2 + 1 - core, away(acc, ka, acc_size))))

    relays_one(0)
    relays_one(1)
    relays_two(0)
    relays_three(0)
    relays_two(1)
    relays_four(0)
    relays_three(1)

    def sites_of(kind, rank, which, n, size):
        at = core if which == 0 else 1 - core
        rows = [land[kind][pl.ds((k * 2 + at) * acc_size, acc_size)].reshape(don_sites, width) for k in range(chips)]
        ranks = [
            jnp.where(
                at == 0,
                rank[:, 2 * k * don_sites : (2 * k + 1) * don_sites],
                rank[:, (2 * k + 1) * don_sites : (2 * k + 2) * don_sites],
            )
            for k in range(chips)
        ]
        row = lax.broadcasted_iota(I32, (size, sites // 2), 0) + n
        pick = jnp.where(row == jnp.concatenate(ranks, axis=1), 1.0, 0.0).astype(BF16)
        return jnp.dot(pick, jnp.concatenate(rows, axis=0), preferred_element_type=F32)

    for copy in side:
        copy.wait()
    counts = cnt_l[0]
    for k in range(1, don_size):
        counts = counts + cnt_l[k]
    counts = counts.astype(BF16)
    first = jnp.dot(counts, first_s[0], preferred_element_type=F32)
    number = jnp.dot(counts, first_s[1], preferred_element_type=F32)
    shard_of = jnp.sum(first_s[0].astype(F32), axis=0, keepdims=True)
    within = lax.broadcasted_iota(I32, (8, sites), 1).astype(F32) - shard_of * slots
    rank_d = jnp.where(within < number, first + within, -1.0).astype(I32)[:1]
    comb = jnp.concatenate([comb_l[k] for k in range(don_size)], axis=1)
    table = jnp.concatenate(
        [(comb & 1).astype(F32), ((comb >> 1) & 255).astype(F32), (comb >> 9).astype(F32)], axis=0
    ).astype(BF16)
    stage_four(0)
    for n in range(0, rows_live, chunk):
        size = min(chunk, rows_live - n)
        span = slice(n, n + size)
        row = lax.broadcasted_iota(I32, (size, sites), 0) + n
        pick = jnp.where(row == rank_d, 1.0, 0.0).astype(BF16)
        d = jnp.dot(pick, xd[...].reshape(sites, width), preferred_element_type=F32)
        d_s[span, :] = d.astype(BF16)
        tab_s[:, span] = contract_last(table, pick)

    weights_in[0].wait()

    def project(t):
        for n in range(0, rows_live, chunk):
            span = slice(n, min(n + chunk, rows_live))
            p_s[t, span, :] = jnp.dot(d_s[span, :], w_s[t], preferred_element_type=F32).astype(BF16)

    for t in range(half):
        if t == half // 2:
            relays_four(1)
        project(t)
    for n in range(0, rows_d, chunk):
        span = slice(n, n + chunk)
        dt_s[:, span] = jnp.transpose(d_s[span, :].astype(F32)).astype(BF16)

    for which in range(2):
        if which:
            stage_four(1)
        for n in range(0, rows_live, chunk):
            size = min(chunk, rows_live - n)
            rows = sites_of(1, rank_s[:1, :], which, n, size)
            if which:
                rows = rows + a_s[n : n + size, :].astype(F32)
            a_s[n : n + size, :] = rows.astype(BF16)

    label_col = jnp.transpose(jnp.broadcast_to(label_s[:1, :rows_a].astype(F32), (128, rows_a)))[:rows_live]
    lost = []
    kept = []

    group = comb_s.shape[1]

    def hits(t, span):
        goal = tab_s[pl.ds(group + t, 1), span] + 256.0 * tab_s[pl.ds(2 * group + t, 1), span]
        return jnp.concatenate([label_col] * (chunk // 128), axis=1) == goal

    deep = e_s.shape[0]

    def score(t):
        for n in range(0, rows_d, chunk):
            span = slice(n, n + chunk)
            raw = contract_last(a_s[:rows_live, :], p_s[t, span, :])
            if rows_live > live:
                row = lax.broadcasted_iota(I32, raw.shape, 0)
                raw = jnp.where(row < live, raw, -1e30)
            weight = tab_s[pl.ds(t, 1), span]
            highest = jnp.max(raw, axis=0, keepdims=True)
            expo = jnp.exp2((raw - highest) * (scale * LOG2E))
            e_s[t % deep, :, span] = expo
            summed = jnp.sum(expo, axis=0, keepdims=True)
            picked = jnp.sum(jnp.where(hits(t, span), raw, 0.0), axis=0, keepdims=True)
            lost.append(weight * (jnp.log(summed) + scale * (highest - picked)))
            kept.append((t, span, weight, weight / summed))
    at_loss = core * acc_size + acc
    loss_copies = []

    def send_loss():
        def lanes(parts):
            whole = sum(parts[1:], parts[0])
            pieces = [whole[:, n : n + 128] for n in range(0, whole.shape[1], 128)]
            return sum(pieces[1:], pieces[0])

        num, cnt = lanes(lost), lanes([weight for _, _, weight, _ in kept])
        first_row = lax.broadcasted_iota(I32, loss_s.shape, 0) == 0
        loss_s[...] = jnp.where(first_row, num, cnt)
        for k, peer in enumerate(lossers):
            copy = pltpu.make_async_remote_copy(
                src_ref=loss_s, dst_ref=loss_l.at[at_loss], send_sem=loss_send.at[k], recv_sem=loss_recv.at[at_loss],
                device_id=peer, device_id_type=MESH,
            )
            copy.start()
            loss_copies.append(copy)
        loss_l[at_loss] = loss_s[...]

    tot_copies = []

    def back(t):
        for t_at, span, weight, factor in kept:
            if t_at == t:
                prob = e_s[t % deep, :, span] * factor
                ds_s[t % deep, :rows_live, span] = jnp.where(hits(t, span), prob - weight, prob).astype(BF16)
        at = core * half + t
        for mine in (False, True):
            which = core if mine else 1 - core
            rows = pl.multiple_of((x * 2 + which) * depth, depth)
            total = contract_last(dt_s[pl.ds(rows, depth), :], ds_s[t % deep]) * scale
            if mine:
                tot_out[at] = total.astype(BF16)
            else:
                tot_s[t] = total.astype(BF16)
                copy = pltpu.make_async_remote_copy(
                    src_ref=tot_s.at[t], dst_ref=tot_out.at[at], send_sem=tot_send.at[t], recv_sem=tot_recv.at[t],
                    device_id=sibling, device_id_type=MESH,
                )
                copy.start()
                tot_copies.append(copy)

    for first in range(0, half, deep):
        for t in range(first, first + deep):
            score(t)
            if t == half - 1:
                send_loss()
        for t in range(first, first + deep):
            back(t)

    def gradient(at):
        grad_out[at] = jnp.dot(tot_out[at], a_s[...], preferred_element_type=F32)

    for t in range(half):
        gradient(core * half + t)
    for t in range(half):
        tot_copies[t].wait()
        gradient((1 - core) * half + t)
    for copy in sent:
        copy.wait_send()
    for copy in loss_copies:
        copy.wait_send()
    for peer in lossers:
        source = lax.rem(peer[0], 2) * acc_size + peer[1]
        pltpu.make_async_copy(loss_s, loss_l.at[source], loss_recv.at[source]).wait()
    total = loss_l[0]
    for k in range(1, 2 * acc_size):
        total = total + loss_l[k]
    total = jnp.sum(total, axis=1, keepdims=True)
    loss_out[...] = jnp.broadcast_to(total[:1] / jnp.maximum(total[1:2], 1.0), loss_out.shape)


def main(don_size, acc_size, dpos, apos, dcnt, acnt, demb, aemb, target, mask, weights):
    slots, width = dpos.shape[0], demb.shape[1]
    tis = weights.shape[0]
    half = tis // 2
    shards = don_size * acc_size
    sites = shards * slots
    live = shards * (slots + 1) // 2
    padded = round_up(live, 128)
    depth = width // don_size
    inner = 1
    while (2 * inner) ** 2 <= acc_size:
        inner *= 2
    outer, chips = acc_size // inner, don_size // 2
    sends = shards // 2 + (outer - 1) + outer * inner * chips - outer
    tile_rows = max(8, tis)
    hbm = pl.BlockSpec(memory_space=pltpu.HBM)
    vmem = pl.BlockSpec(memory_space=pltpu.VMEM)
    dma = pltpu.SemaphoreType.DMA
    lossers = 2 * acc_size - 1
    deep = half if half * padded * padded <= 1 << 21 else 1
    arrays = 2 * width * (2 * demb.shape[0] + half * width + 3 * sites + (3 + half) * padded + tis * depth)
    limit = arrays + arrays // 4 + deep * padded * padded * 6 + (8 << 20)
    return pl.pallas_call(
        functools.partial(main_kernel, don_size, acc_size, inner, live),
        in_specs=[hbm] * 9,
        out_specs=[vmem, vmem],
        out_shape=[
            jax.ShapeDtypeStruct((tis, depth, width), F32),
            jax.ShapeDtypeStruct((8, 128), F32),
        ],
        scratch_shapes=[
            pltpu.SMEM(dpos.shape, I32),
            pltpu.SMEM(apos.shape, I32),
            pltpu.SMEM(dcnt.shape, I32),
            pltpu.SMEM(acnt.shape, I32),
            pltpu.VMEM(demb.shape, BF16),
            pltpu.VMEM(aemb.shape, BF16),
            pltpu.VMEM((half, width, width), BF16),
            pltpu.VMEM((2, tile_rows, sites // don_size), I32),
            pltpu.VMEM((shards, slots, width), BF16),
            pltpu.VMEM((shards, slots, width), BF16),
            pltpu.VMEM((2, max(8, half), sites // don_size), I32),
            pltpu.VMEM((don_size, max(8, half), sites // don_size), I32),
            pltpu.VMEM((8, 128), F32),
            pltpu.VMEM((don_size, 8, 128), F32),
            pltpu.VMEM((padded, width), BF16),
            pltpu.VMEM((width, padded), BF16),
            pltpu.VMEM((padded, width), BF16),
            pltpu.VMEM((half, padded, width), BF16),
            pltpu.VMEM((deep, round_up(live, 16), padded), F32),
            pltpu.VMEM((deep, padded, padded), BF16),
            pltpu.VMEM((tis, depth, padded), BF16),
            pltpu.VMEM((half, depth, padded), BF16),
            pltpu.VMEM((8, sites), I32),
            pltpu.VMEM((8, sites), I32),
            pltpu.VMEM((3 * max(8, half), padded), F32),
            pltpu.VMEM((2, 128, sites), BF16),
            pltpu.VMEM((8, 128), F32),
            pltpu.VMEM((2 * acc_size, 8, 128), F32),
            dma((9,)),
            dma((half,)),
            dma((2, PIECES)),
            dma((2, sends)),
            dma((2, shards)),
            dma((1,)),
            dma((1,)),
            dma((don_size - 1, 2)),
            dma((don_size - 1, 2)),
            dma((half,)),
            dma((half,)),
            dma((lossers,)),
            dma((lossers + 1,)),
        ],
        compiler_params=pltpu.CompilerParams(
            collective_id=0, has_side_effects=True, vmem_limit_bytes=min(limit, 60 << 20)
        ),
    )(*[
        pltpu.with_memory_space_constraint(array, pltpu.HBM)
        for array in (dpos, apos, dcnt, acnt, demb, aemb, target, mask, weights)
    ])


def grad_kernel(buf, loss_ref, grad_ref, out_ref, sem):
    copies = []
    for t in range(buf.shape[0]):
        copy = pltpu.make_async_copy(buf.at[t], grad_ref.at[:, t, :], sem.at[t])
        copy.start()
        copies.append(copy)
    out_ref[0, 0] = jnp.max(loss_ref[...])
    for copy in copies:
        copy.wait()


def grad(by_tissue, loss):
    tis, depth, width = by_tissue.shape
    vmem = pl.BlockSpec(memory_space=pltpu.VMEM)
    return pl.pallas_call(
        grad_kernel,
        in_specs=[vmem, vmem],
        out_specs=[pl.BlockSpec(memory_space=pl.ANY), pl.BlockSpec(memory_space=pltpu.SMEM)],
        out_shape=[jax.ShapeDtypeStruct((depth, tis, width), F32), jax.ShapeDtypeStruct((1, 1), F32)],
        scratch_shapes=[pltpu.SemaphoreType.DMA((tis,))],
        compiler_params=pltpu.CompilerParams(vmem_limit_bytes=8 << 20),
    )(by_tissue, loss)


def local(
    don_size, acc_size, donor_emb, acceptor_emb, donor_pos, acceptor_pos, donor_count, acceptor_count,
    target, junction_mask, weights,
):
    by_tissue, loss = main(
        don_size, acc_size, donor_pos, acceptor_pos, donor_count, acceptor_count,
        donor_emb, acceptor_emb, target, junction_mask, weights,
    )
    grad_weight, loss = grad(by_tissue, loss)
    return loss.reshape(()), grad_weight


def solution(mesh):
    return jax.shard_map(
        functools.partial(local, mesh.shape["don"], mesh.shape["acc"]),
        mesh=mesh,
        in_specs=(
            P(("don", "acc"), None),
            P(("don", "acc"), None),
            P(("don", "acc")),
            P(("don", "acc")),
            P("don"),
            P(),
            P(None, "don"),
            P(None, "don"),
            P("acc", None, None),
        ),
        out_specs=(P(), P("don", "acc", None)),
        check_vma=False,
    )
```

```python
import functools
import itertools
import math

import jax
import jax.numpy as jnp
from jax import lax
from jax.experimental import pallas as pl
from jax.experimental.pallas import tpu as pltpu
from jax.sharding import PartitionSpec as P

BF16 = jnp.bfloat16
F32 = jnp.float32
I32 = jnp.int32
MESH = pl.DeviceIdType.MESH
PIECES = 4
LOG2E = 1.4426950408889634


def round_up(n, m):
    return (n + m - 1) // m * m


def row_chunk(n, limit=512):
    best = 128
    for r in range(128, limit + 1, 128):
        if n % r == 0:
            best = r
    return best


def contract_last(a, b):
    return lax.dot_general(a, b, (((1,), (1,)), ((), ())), preferred_element_type=F32)


def acceptor_tables(counts, shards, slots, width):
    col = lax.broadcasted_iota(I32, (8, width), 1)

    def step(k, carry):
        first, rank, label = carry
        number = counts[k]
        within = col - k * slots
        live = (within >= 0) & (within < number)
        rank = jnp.where(live, first + within, rank)
        last = first + number
        return last, rank, label + jnp.where(col >= last, slots - number, 0)

    return lax.fori_loop(0, shards, step, (jnp.int32(0), jnp.full((8, width), -1, I32), col))[1:]


def main_kernel(
    don_size, acc_size, inner, live,
    dpos_h, apos_h, dcnt_h, acnt_h, demb, aemb, target, mask, weights,
    grad_out, loss_out,
    dpos, apos, dcnt, acnt, demb_v, aemb_v, w_s, tm_s, xd, xa, comb_s, comb_l, cnt_s, cnt_l,
    d_s, dt_s, a_s, p_s, e_s, ds_s, tot_out, tot_s, rank_s, label_s, tab_s, first_s, loss_s, loss_l,
    in_sem, w_sem, row_sem, send_sem, recv_sem, sib_send, sib_recv, side_send, side_recv,
    tot_send, tot_recv, loss_send, loss_recv,
):
    shards, slots, width = xd.shape
    outer, chips = acc_size // inner, don_size // 2
    sites = shards * slots
    don_sites = sites // don_size
    half, rows_d = w_s.shape[0], d_s.shape[0]
    rows_a = a_s.shape[0]
    depth = width // don_size
    tis = 2 * half
    scale = width ** (-0.5)
    alternate = chips == inner
    don, acc = lax.axis_index("don"), lax.axis_index("acc")
    core, x = lax.rem(don, 2), don // 2
    o, i = acc // inner, lax.rem(acc, inner)
    if alternate:
        b = core * x + (1 - core) * i
        c = core * i + (1 - core) * x
        b_size, c_size = inner, inner
    else:
        b, c, b_size, c_size = i, x, inner, chips

    def place(oo, bb, cc):
        if alternate:
            xx = core * bb + (1 - core) * cc
            ii = core * cc + (1 - core) * bb
        else:
            xx, ii = cc, bb
        return (xx * 2 + core, oo * inner + ii)

    def away(at, k, size):
        return lax.rem(at + k, size)

    def near(at, k, size):
        up = k - 1 + jnp.where(k - 1 >= at, 1, 0)
        down = k - 1 + jnp.where(k - 1 >= size - 1 - at, 1, 0)
        return jnp.where(2 * at < size, up, size - 1 - down)

    def slot_of(at):
        return at[0] * acc_size + at[1]

    sibling = (x * 2 + 1 - core, acc)
    tile_rows = tm_s.shape[1]
    row_at = pl.multiple_of(acc * tis // tile_rows * tile_rows, tile_rows)
    copies = [
        None,
        pltpu.make_async_copy(target.at[pl.ds(row_at, tile_rows), :], tm_s.at[0], in_sem.at[1]),
        pltpu.make_async_copy(mask.at[pl.ds(row_at, tile_rows), :], tm_s.at[1], in_sem.at[2]),
        None,
        None,
    ]
    weights_in = [pltpu.make_async_copy(weights.at[pl.ds(core * half, half)], w_s, w_sem.at[0])]
    small = [
        pltpu.make_async_copy(source, dest, in_sem.at[5 + k])
        for k, (source, dest) in enumerate(((dpos_h, dpos), (apos_h, apos), (dcnt_h, dcnt), (acnt_h, acnt)))
    ]
    piece = demb_v.shape[0] // PIECES
    rows_in = [
        [
            pltpu.make_async_copy(
                emb.at[pl.ds(n * piece, piece), :], emb_v.at[pl.ds(n * piece, piece), :], row_sem.at[which, n]
            )
            for n in range(PIECES)
        ]
        for which, (emb, emb_v) in enumerate(((demb, demb_v), (aemb, aemb_v)))
    ]
    for copy in small[:2] + rows_in[0] + small[2:] + copies[1:3]:
        copy.start()

    others = [(away(don, k, don_size), acc) for k in range(1, don_size)]
    lossers = [
        (x * 2 + away(core, kc, 2), (near(o, ko, outer) if ko else o) * inner + away(i, ki, inner))
        for ko in range(outer - 1, -1, -1) for ki in range(inner - 1, -1, -1) for kc in (1, 0) if ko or ki or kc
    ]
    direct = others + [(don, away(o, k, outer) * inner + i) for k in range(1, outer)]
    direct += [(don, o * inner + away(i, k, inner)) for k in range(1, inner)]
    barrier = pltpu.get_barrier_semaphore()
    for peer in direct:
        pl.semaphore_signal(barrier, inc=1, device_id=peer, device_id_type=MESH)

    def own_rows(pos, which, landing):
        emb_v = (demb_v, aemb_v)[which]
        small[which].wait()
        row = lax.broadcasted_iota(I32, (slots, 128), 0)
        want = jnp.zeros((slots, 128), I32)
        for k in range(slots):
            want = jnp.where(row == k, pos[k], want)
        col = lax.broadcasted_iota(I32, (slots, piece), 1)
        want = jnp.concatenate([want] * (piece // 128), axis=1)
        rows = jnp.zeros((slots, width), F32)
        for n in range(PIECES):
            pick = jnp.where(col + n * piece == want, 1.0, 0.0).astype(BF16)
            rows_in[which][n].wait()
            rows = rows + jnp.dot(pick, emb_v[n * piece : (n + 1) * piece, :], preferred_element_type=F32)
        landing[held] = rows.astype(BF16)

    held = don * acc_size + acc
    own_rows(dpos, 0, xd)
    pl.semaphore_wait(barrier, len(direct))

    sent = []
    land = (xd, xa)

    def send(kind, source, slot, peer, count):
        n = count[kind]
        count[kind] += 1
        copy = pltpu.make_async_remote_copy(
            src_ref=source, dst_ref=land[kind].at[slot],
            send_sem=send_sem.at[kind, n], recv_sem=recv_sem.at[kind, slot],
            device_id=peer, device_id_type=MESH,
        )
        copy.start()
        sent.append(copy)

    def arrived(kind, slot):
        pltpu.make_async_copy(land[kind].at[slot], land[kind].at[slot], recv_sem.at[kind, slot]).wait()

    counter = [0, 0]

    def at_offset(ko, kb, kc):
        return place(near(o, ko, outer) if ko else o, away(b, kb, b_size), away(c, kc, c_size))

    def targets(ko, kb, kc):
        line = [(k, 0, 0) for k in range(outer - 1, 0, -1)]
        along_b = [(0, k, 0) for k in range(1, b_size)]
        along_c = [(0, 0, k) for k in range(1, c_size)]
        return [] if kc else along_c if kb else along_b + along_c if ko else line + along_b + along_c

    def forward(kind, offset):
        slot = slot_of(at_offset(*offset))
        for hop in targets(*offset):
            send(kind, land[kind].at[slot], slot, at_offset(*hop), counter)
        send(kind, land[kind].at[slot], slot, sibling, counter)

    def relay(kind, offset):
        arrived(kind, slot_of(at_offset(*offset)))
        forward(kind, offset)

    every = list(itertools.product(range(outer), range(b_size), range(c_size)))
    relayed = set()

    def relays(kind, chosen):
        for offset in every:
            if any(offset) and chosen(*offset) and (kind, offset) not in relayed:
                relayed.add((kind, offset))
                relay(kind, offset)

    def relays_one(kind):
        relays(kind, lambda ko, kb, kc: not ko and not kc)
        relays(kind, lambda ko, kb, kc: not kb and not kc)

    def relays_two(kind):
        relays(kind, lambda ko, kb, kc: ko and not kc)

    def relays_three(kind):
        relays(kind, lambda ko, kb, kc: not kb)

    def relays_four(kind):
        relays(kind, lambda ko, kb, kc: True)

    forward(0, (0, 0, 0))
    for copy in rows_in[1]:
        copy.start()
    own_rows(apos, 1, xa)
    forward(1, (0, 0, 0))
    for copy in weights_in:
        copy.start()
    copies[1].wait()
    copies[2].wait()
    both = tm_s[0] * 2 + tm_s[1]
    for core_at in range(2):
        mine = both[core_at * half : (core_at + 1) * half]
        for k in range(1, tile_rows // tis):
            at = k * tis + core_at * half
            mine = jnp.where(lax.rem(acc, tile_rows // tis) == k, both[at : at + half], mine)
        comb_s[core_at] = jnp.concatenate([mine] * (comb_s.shape[1] // half), axis=0)

    for copy in small[2:]:
        copy.wait()
    lane = lax.broadcasted_iota(I32, (1, 128), 1)
    counts = jnp.zeros((1, 128), F32)
    for k in range(shards // don_size):
        counts = jnp.where(lane == don * (shards // don_size) + k, dcnt[k].astype(F32), counts)
    cnt_s[...] = jnp.broadcast_to(counts, cnt_s.shape)
    side = []
    for k, peer in enumerate(others):
        to = lax.rem(peer[0], 2)
        for j, (source, dest) in enumerate(((comb_s.at[to], comb_l.at[don]), (cnt_s, cnt_l.at[don]))):
            copy = pltpu.make_async_remote_copy(
                src_ref=source, dst_ref=dest, send_sem=side_send.at[k, j], recv_sem=side_recv.at[k, j],
                device_id=peer, device_id_type=MESH,
            )
            copy.start()
            side.append(copy)
    comb_l[don] = comb_s[core]
    cnt_l[don] = cnt_s[...]

    rank_a, label_a = acceptor_tables(acnt, shards, slots, sites)
    rank_s[...] = rank_a
    label_s[...] = label_a
    shard_row = lax.broadcasted_iota(I32, (first_s.shape[1], sites), 0)
    slot_lane = lax.broadcasted_iota(I32, (first_s.shape[1], sites), 1)
    before = slot_lane >= (shard_row + 1) * slots
    within_shard = (slot_lane >= shard_row * slots) & jnp.logical_not(before)
    first_s[0] = jnp.where(before, 1.0, 0.0).astype(BF16)
    first_s[1] = jnp.where(within_shard, 1.0, 0.0).astype(BF16)

    rows_live = round_up(live, 16)
    chunk = row_chunk(rows_d)
    if rows_a > rows_live:
        a_s[rows_live:, :] = jnp.zeros((rows_a - rows_live, width), BF16)
        d_s[rows_live:, :] = jnp.zeros((rows_d - rows_live, width), BF16)
        tab_s[:, rows_live:] = jnp.zeros((tab_s.shape[0], rows_d - rows_live), F32)
        for t in range(half):
            p_s[t, rows_live:, :] = jnp.zeros((rows_d - rows_live, width), BF16)
        for t in range(ds_s.shape[0]):
            ds_s[t, rows_live:, :] = jnp.zeros((rows_a - rows_live, rows_d), BF16)


    def stage_four(kind):
        for kx in range(chips):
            for ka in range(acc_size):
                arrived(kind, slot_of((away(x, kx, chips) * 2 + 1 - core, away(acc, ka, acc_size))))

    relays_one(0)
    relays_one(1)
    relays_two(0)
    relays_three(0)
    relays_two(1)
    relays_four(0)
    relays_three(1)

    def sites_of(kind, rank, which, n, size):
        at = core if which == 0 else 1 - core
        rows = [land[kind][pl.ds((k * 2 + at) * acc_size, acc_size)].reshape(don_sites, width) for k in range(chips)]
        ranks = [
            jnp.where(
                at == 0,
                rank[:, 2 * k * don_sites : (2 * k + 1) * don_sites],
                rank[:, (2 * k + 1) * don_sites : (2 * k + 2) * don_sites],
            )
            for k in range(chips)
        ]
        row = lax.broadcasted_iota(I32, (size, sites // 2), 0) + n
        pick = jnp.where(row == jnp.concatenate(ranks, axis=1), 1.0, 0.0).astype(BF16)
        return jnp.dot(pick, jnp.concatenate(rows, axis=0), preferred_element_type=F32)

    for copy in side:
        copy.wait()
    counts = cnt_l[0]
    for k in range(1, don_size):
        counts = counts + cnt_l[k]
    counts = counts.astype(BF16)
    first = jnp.dot(counts, first_s[0], preferred_element_type=F32)
    number = jnp.dot(counts, first_s[1], preferred_element_type=F32)
    shard_of = jnp.sum(first_s[0].astype(F32), axis=0, keepdims=True)
    within = lax.broadcasted_iota(I32, (8, sites), 1).astype(F32) - shard_of * slots
    rank_d = jnp.where(within < number, first + within, -1.0).astype(I32)[:1]
    comb = jnp.concatenate([comb_l[k] for k in range(don_size)], axis=1)
    table = jnp.concatenate(
        [(comb & 1).astype(F32), ((comb >> 1) & 255).astype(F32), (comb >> 9).astype(F32)], axis=0
    ).astype(BF16)
    stage_four(0)
    for n in range(0, rows_live, chunk):
        size = min(chunk, rows_live - n)
        span = slice(n, n + size)
        row = lax.broadcasted_iota(I32, (size, sites), 0) + n
        pick = jnp.where(row == rank_d, 1.0, 0.0).astype(BF16)
        d = jnp.dot(pick, xd[...].reshape(sites, width), preferred_element_type=F32)
        d_s[span, :] = d.astype(BF16)
        tab_s[:, span] = contract_last(table, pick)

    weights_in[0].wait()

    def project(t):
        for n in range(0, rows_live, chunk):
            span = slice(n, min(n + chunk, rows_live))
            p_s[t, span, :] = jnp.dot(d_s[span, :], w_s[t], preferred_element_type=F32).astype(BF16)

    for t in range(half):
        if t == half // 2:
            relays_four(1)
        project(t)
    def transpose_donors():
        for n in range(0, rows_d, chunk):
            span = slice(n, n + chunk)
            dt_s[:, span] = jnp.transpose(d_s[span, :].astype(F32)).astype(BF16)

    if e_s.shape[0] < half:
        transpose_donors()

    label_col = jnp.transpose(jnp.broadcast_to(label_s[:1, :rows_a].astype(F32), (128, rows_a)))[:rows_live]
    for which in range(2):
        if which:
            stage_four(1)
        for n in range(0, rows_live, chunk):
            size = min(chunk, rows_live - n)
            rows = sites_of(1, rank_s[:1, :], which, n, size)
            if which:
                rows = rows + a_s[n : n + size, :].astype(F32)
            a_s[n : n + size, :] = rows.astype(BF16)

    lost = []
    kept = []

    group = comb_s.shape[1]

    def hits(t, span):
        goal = tab_s[pl.ds(group + t, 1), span] + 256.0 * tab_s[pl.ds(2 * group + t, 1), span]
        return jnp.concatenate([label_col] * (chunk // 128), axis=1) == goal

    deep = e_s.shape[0]

    def score(t):
        for n in range(0, rows_d, chunk):
            span = slice(n, n + chunk)
            raw = contract_last(a_s[:rows_live, :], p_s[t, span, :])
            if rows_live > live:
                row = lax.broadcasted_iota(I32, raw.shape, 0)
                raw = jnp.where(row < live, raw, -1e30)
            weight = tab_s[pl.ds(t, 1), span]
            highest = jnp.max(raw, axis=0, keepdims=True)
            expo = jnp.exp2((raw - highest) * (scale * LOG2E))
            e_s[t % deep, :, span] = expo
            summed = jnp.sum(expo, axis=0, keepdims=True)
            picked = jnp.sum(jnp.where(hits(t, span), raw, 0.0), axis=0, keepdims=True)
            lost.append(weight * (jnp.log(summed) + scale * (highest - picked)))
            kept.append((t, span, weight, weight / summed))
    at_loss = core * acc_size + acc
    loss_copies = []

    def send_loss():
        def lanes(parts):
            whole = sum(parts[1:], parts[0])
            pieces = [whole[:, n : n + 128] for n in range(0, whole.shape[1], 128)]
            return sum(pieces[1:], pieces[0])

        num, cnt = lanes(lost), lanes([weight for _, _, weight, _ in kept])
        first_row = lax.broadcasted_iota(I32, loss_s.shape, 0) == 0
        loss_s[...] = jnp.where(first_row, num, cnt)
        for k, peer in enumerate(lossers):
            copy = pltpu.make_async_remote_copy(
                src_ref=loss_s, dst_ref=loss_l.at[at_loss], send_sem=loss_send.at[k], recv_sem=loss_recv.at[at_loss],
                device_id=peer, device_id_type=MESH,
            )
            copy.start()
            loss_copies.append(copy)
        loss_l[at_loss] = loss_s[...]

    tot_copies = []

    def back(t):
        for t_at, span, weight, factor in kept:
            if t_at == t:
                prob = e_s[t % deep, :, span] * factor
                ds_s[t % deep, :rows_live, span] = jnp.where(hits(t, span), prob - weight, prob).astype(BF16)
        at = core * half + t
        for mine in (False, True):
            which = core if mine else 1 - core
            rows = pl.multiple_of((x * 2 + which) * depth, depth)
            total = contract_last(dt_s[pl.ds(rows, depth), :], ds_s[t % deep]) * scale
            if mine:
                tot_out[at] = total.astype(BF16)
            else:
                tot_s[t] = total.astype(BF16)
                copy = pltpu.make_async_remote_copy(
                    src_ref=tot_s.at[t], dst_ref=tot_out.at[at], send_sem=tot_send.at[t], recv_sem=tot_recv.at[t],
                    device_id=sibling, device_id_type=MESH,
                )
                copy.start()
                tot_copies.append(copy)

    for first in range(0, half, deep):
        for t in range(first, first + deep):
            score(t)
            if t == half - 1:
                send_loss()
                if deep == half:
                    transpose_donors()
        for t in range(first, first + deep):
            back(t)

    def gradient(at):
        grad_out[at] = jnp.dot(tot_out[at], a_s[...], preferred_element_type=F32)

    for t in range(half):
        gradient(core * half + t)
    for t in range(half):
        tot_copies[t].wait()
        gradient((1 - core) * half + t)
    for copy in sent:
        copy.wait_send()
    for copy in loss_copies:
        copy.wait_send()
    for peer in lossers:
        source = lax.rem(peer[0], 2) * acc_size + peer[1]
        pltpu.make_async_copy(loss_s, loss_l.at[source], loss_recv.at[source]).wait()
    total = loss_l[0]
    for k in range(1, 2 * acc_size):
        total = total + loss_l[k]
    total = jnp.sum(total, axis=1, keepdims=True)
    loss_out[...] = jnp.broadcast_to(total[:1] / jnp.maximum(total[1:2], 1.0), loss_out.shape)


def main(don_size, acc_size, dpos, apos, dcnt, acnt, demb, aemb, target, mask, weights):
    slots, width = dpos.shape[0], demb.shape[1]
    tis = weights.shape[0]
    half = tis // 2
    shards = don_size * acc_size
    sites = shards * slots
    live = shards * (slots + 1) // 2
    padded = round_up(live, 128)
    depth = width // don_size
    inner = 1
    while (2 * inner) ** 2 <= acc_size:
        inner *= 2
    outer, chips = acc_size // inner, don_size // 2
    sends = shards // 2 + (outer - 1) + outer * inner * chips - outer
    tile_rows = max(8, tis)
    hbm = pl.BlockSpec(memory_space=pltpu.HBM)
    vmem = pl.BlockSpec(memory_space=pltpu.VMEM)
    dma = pltpu.SemaphoreType.DMA
    lossers = 2 * acc_size - 1
    deep = half if half * padded * padded <= 1 << 21 else 1
    arrays = 2 * width * (2 * demb.shape[0] + half * width + 3 * sites + (3 + half) * padded + tis * depth)
    limit = arrays + arrays // 4 + deep * padded * padded * 6 + (8 << 20)
    return pl.pallas_call(
        functools.partial(main_kernel, don_size, acc_size, inner, live),
        in_specs=[hbm] * 9,
        out_specs=[vmem, vmem],
        out_shape=[
            jax.ShapeDtypeStruct((tis, depth, width), F32),
            jax.ShapeDtypeStruct((8, 128), F32),
        ],
        scratch_shapes=[
            pltpu.SMEM(dpos.shape, I32),
            pltpu.SMEM(apos.shape, I32),
            pltpu.SMEM(dcnt.shape, I32),
            pltpu.SMEM(acnt.shape, I32),
            pltpu.VMEM(demb.shape, BF16),
            pltpu.VMEM(aemb.shape, BF16),
            pltpu.VMEM((half, width, width), BF16),
            pltpu.VMEM((2, tile_rows, sites // don_size), I32),
            pltpu.VMEM((shards, slots, width), BF16),
            pltpu.VMEM((shards, slots, width), BF16),
            pltpu.VMEM((2, max(8, half), sites // don_size), I32),
            pltpu.VMEM((don_size, max(8, half), sites // don_size), I32),
            pltpu.VMEM((8, 128), F32),
            pltpu.VMEM((don_size, 8, 128), F32),
            pltpu.VMEM((padded, width), BF16),
            pltpu.VMEM((width, padded), BF16),
            pltpu.VMEM((padded, width), BF16),
            pltpu.VMEM((half, padded, width), BF16),
            pltpu.VMEM((deep, round_up(live, 16), padded), F32),
            pltpu.VMEM((deep, padded, padded), BF16),
            pltpu.VMEM((tis, depth, padded), BF16),
            pltpu.VMEM((half, depth, padded), BF16),
            pltpu.VMEM((8, sites), I32),
            pltpu.VMEM((8, sites), I32),
            pltpu.VMEM((3 * max(8, half), padded), F32),
            pltpu.VMEM((2, 128, sites), BF16),
            pltpu.VMEM((8, 128), F32),
            pltpu.VMEM((2 * acc_size, 8, 128), F32),
            dma((9,)),
            dma((half,)),
            dma((2, PIECES)),
            dma((2, sends)),
            dma((2, shards)),
            dma((1,)),
            dma((1,)),
            dma((don_size - 1, 2)),
            dma((don_size - 1, 2)),
            dma((half,)),
            dma((half,)),
            dma((lossers,)),
            dma((lossers + 1,)),
        ],
        compiler_params=pltpu.CompilerParams(
            collective_id=0, has_side_effects=True, vmem_limit_bytes=min(limit, 60 << 20)
        ),
    )(*[
        pltpu.with_memory_space_constraint(array, pltpu.HBM)
        for array in (dpos, apos, dcnt, acnt, demb, aemb, target, mask, weights)
    ])


def grad_kernel(buf, loss_ref, grad_ref, out_ref, sem):
    copies = []
    for t in range(buf.shape[0]):
        copy = pltpu.make_async_copy(buf.at[t], grad_ref.at[:, t, :], sem.at[t])
        copy.start()
        copies.append(copy)
    out_ref[0, 0] = jnp.max(loss_ref[...])
    for copy in copies:
        copy.wait()


def grad(by_tissue, loss):
    tis, depth, width = by_tissue.shape
    vmem = pl.BlockSpec(memory_space=pltpu.VMEM)
    return pl.pallas_call(
        grad_kernel,
        in_specs=[vmem, vmem],
        out_specs=[pl.BlockSpec(memory_space=pl.ANY), pl.BlockSpec(memory_space=pltpu.SMEM)],
        out_shape=[jax.ShapeDtypeStruct((depth, tis, width), F32), jax.ShapeDtypeStruct((1, 1), F32)],
        scratch_shapes=[pltpu.SemaphoreType.DMA((tis,))],
        compiler_params=pltpu.CompilerParams(vmem_limit_bytes=8 << 20),
    )(by_tissue, loss)


def local(
    don_size, acc_size, donor_emb, acceptor_emb, donor_pos, acceptor_pos, donor_count, acceptor_count,
    target, junction_mask, weights,
):
    by_tissue, loss = main(
        don_size, acc_size, donor_pos, acceptor_pos, donor_count, acceptor_count,
        donor_emb, acceptor_emb, target, junction_mask, weights,
    )
    grad_weight, loss = grad(by_tissue, loss)
    return loss.reshape(()), grad_weight


def solution(mesh):
    return jax.shard_map(
        functools.partial(local, mesh.shape["don"], mesh.shape["acc"]),
        mesh=mesh,
        in_specs=(
            P(("don", "acc"), None),
            P(("don", "acc"), None),
            P(("don", "acc")),
            P(("don", "acc")),
            P("don"),
            P(),
            P(None, "don"),
            P(None, "don"),
            P("acc", None, None),
        ),
        out_specs=(P(), P("don", "acc", None)),
        check_vma=False,
    )
```
